256 devices in a mesh: gx: 8 (over y, x_hi), gy: 32 (over z, x_lo, core).
Axes of the slice: x: 4 (x_hi: 2, x_lo: 2; x = x_hi * 2 + x_lo), y: 4, z: 8, core: 2. Of those that a mesh axis runs over, the one named last changes fastest.
Arguments:
- positions: float32 [3, 64, 64, 512], P(None, 'gx', 'gy'), may hold values from 0 to 1
- charges: float32 [64, 64, 512], P('gx', 'gy'), may hold values from -0.24 to 0.24
- counts: int32 [64, 64, 8], P('gx', 'gy'), may hold values from 16 to 64, as said below
- up_ops: float32 [3, 296, 296], replicated, may hold values from -0.375 to 0.375
- m2l_ops: float32 [3, 8, 296, 296], replicated, may hold values from -0.125 to 0.125
- down_ops: float32 [2, 2, 296, 296], replicated, may hold values from -0.375 to 0.375
- box_lists: int32 [224, 8], replicated, may hold values from 0 to 127, as said below
Outputs:
- potential: float32 [64, 64, 512], P('gx', 'gy')
The draws below stay inside these ranges and needn't reach their ends.
Inputs may be any that keep to these rules, and one draw needn't show every extreme that they name: `counts`: each leaf holds its particles in its first slots; in every column of 8 leaves along z some leaf is full. `box_lists`: rows o to o + 8 * (32 / 2^h) - 1 belong to level h; entry k of box b there is (b + s) modulo the level's box count, with a shift s of 1 or more that depends on the level and k only; entry 0 has s equal to half the level's box count.
All inputs are finite; a program needn't handle non-finite values.
Results may differ from the reference program's by a relative error of at most 0.0003.
Values sent between devices are 32-bit elements; how exact they have to be, the bound alone decides.
No kernel may reach another device: no remote copies, remote signals or barrier semaphores. Data moves between devices by JAX's collectives and lax.ppermute only.
A program may use at most 64 MiB of HBM per device.

```python
import jax
import jax.numpy as jnp
import numpy as np
from jax import lax

CXL = 8
CYL = 2
LZ = 8
PPL = 64
P_ORD = 8
K = 8
LEV = 3
NE = 296
NXL = 64
NYL = 64
N_GX = 8
N_GY = 32


def draw_counts(key, part):
    key_fill, key_full = jax.random.split(jax.random.fold_in(key, 11))
    filled = jax.random.randint(key_fill, (NXL, NYL, LZ), PPL // 4, PPL + 1)
    full_at = jax.random.randint(key_full, (NXL, NYL, 1), 0, LZ)
    heights = jnp.arange(LZ, dtype=jnp.int32)[None, None, :]
    return jnp.where(heights == full_at, PPL, filled).astype(jnp.int32)


def draw_box_lists(key, part):
    columns = NXL // CXL
    across = NYL // CYL
    stacked = []
    for height in range(1, LEV + 1):
        box_count = columns * (across >> height)
        shifts = jax.random.randint(jax.random.fold_in(key, 100 + height), (1, K), 1, box_count)
        entry_index = jnp.arange(K, dtype=jnp.int32)[None, :]
        shifts = jnp.where(entry_index == 0, box_count // 2, shifts)
        box_index = jnp.arange(box_count, dtype=jnp.int32)[:, None]
        stacked.append((box_index + shifts) % box_count)
    return jnp.concatenate(stacked, axis=0).astype(jnp.int32)


def block_scale(own_key, extent, shards, low, high):
    gain = 1.0
    for dim, parts in shards:
        draws = jax.random.uniform(jax.random.fold_in(jax.random.fold_in(own_key, 6), dim), (parts,), jnp.float32, low / len(shards), high / len(shards))
        gain = gain * jnp.repeat(jnp.exp(draws), extent[dim] // parts).reshape((-1,) + (1,) * (len(extent) - 1 - dim))
    return gain


def noise(key, dims, width, reach, cuts=(), kind=jnp.bfloat16):
    drawn = width * jax.random.normal(key, dims, jnp.float32)
    if cuts:
        drawn = drawn * block_scale(key, dims, cuts, -0.22, 0.18)
    return jnp.clip(drawn, -reach, reach).astype(kind)


def setup_inputs(seed: int = 0) -> dict:
    arg_keys = jax.random.split(jax.random.key(seed), 8)
    return {
        "positions": jnp.clip(1.0 * jax.random.uniform(arg_keys[0], (3, NXL, NYL, LZ * PPL), jnp.float32) ** block_scale(arg_keys[0], (3, NXL, NYL, LZ * PPL), ((1, 8), (2, 32)), -0.2, 0.2), 0.0, 1.0),
        "charges": noise(arg_keys[1], (NXL, NYL, LZ * PPL), 0.03, 0.24, ((0, 8), (1, 32)), jnp.float32),
        "counts": draw_counts(jax.random.fold_in(arg_keys[7], 71), 0),
        "up_ops": noise(arg_keys[3], (LEV, NE, NE), NE ** -0.5, 0.375, (), jnp.float32),
        "m2l_ops": noise(arg_keys[4], (LEV, K, NE, NE), (K * NE) ** -0.5, 0.125, (), jnp.float32),
        "down_ops": noise(arg_keys[5], (LEV - 1, 2, NE, NE), NE ** -0.5, 0.375, (), jnp.float32),
        "box_lists": draw_box_lists(jax.random.fold_in(arg_keys[7], 71), 0),
    }


SOFTENING = 0.01
SURFACE_REACH = 1.05
PRECISE = lax.Precision.HIGHEST

def surface_points(order):
    lattice = np.linspace(-1.0, 1.0, order)
    points_list = []
    for first in range(order):
        for second in range(order):
            for third in range(order):
                if first in (0, order - 1) or second in (0, order - 1) or third in (0, order - 1):
                    points_list.append((lattice[first], lattice[second], lattice[third]))
    return jnp.asarray(np.array(points_list).T, dtype=jnp.float32)

def kernel(gap_x, gap_y, gap_z):
    return lax.rsqrt(gap_x * gap_x + gap_y * gap_y + gap_z * gap_z + SOFTENING)

def live_charges(charges, counts):
    size_x, size_y = (counts.shape[0], counts.shape[1])
    filled = jnp.broadcast_to(counts[..., None], (size_x, size_y, LZ, PPL)).reshape(size_x, size_y, LZ * PPL)
    within = jnp.arange(LZ * PPL, dtype=jnp.int32) % PPL
    occupied = within[None, None, :] < filled
    return (jnp.where(occupied, charges, 0.0), occupied)

def absolute(positions, anchor_x, anchor_y):
    size_x, size_y, slots = (positions.shape[1], positions.shape[2], positions.shape[3])
    along_x = anchor_x + jnp.arange(size_x).astype(jnp.float32)
    along_y = anchor_y + jnp.arange(size_y).astype(jnp.float32)
    along_z = (jnp.arange(slots) // PPL).astype(jnp.float32)
    return jnp.stack([positions[0] + along_x[:, None, None], positions[1] + along_y[None, :, None], positions[2] + along_z[None, None, :]])

def near_field(padded, width_y):
    count_x = padded.shape[1] - 2
    blocks = padded.reshape(4, count_x + 2, width_y + 2, LZ, PPL)
    blocks = jnp.pad(blocks, ((0, 0), (0, 0), (0, 0), (1, 1), (0, 0)))
    rows_in = jnp.arange(PPL)[:, None]
    cols_in = jnp.arange(27 * PPL)[None, :]
    itself = cols_in == rows_in + 13 * PPL

    def one_column(column):
        window = lax.dynamic_slice_in_dim(blocks, column, 3, axis=1)
        target = window[:, 1, 1:-1, 1:-1, :]
        pieces = []
        for shift_x in range(3):
            for shift_y in range(3):
                for shift_z in range(3):
                    source = window[:, shift_x, shift_y:shift_y + width_y, shift_z:shift_z + LZ, :]
                    pieces.append(jnp.stack([source[0] + (shift_x - 1.0), source[1] + (shift_y - 1.0), source[2] + (shift_z - 1.0), source[3]]))
        sources = jnp.concatenate(pieces, axis=-1)
        gap_x = target[0][..., :, None] - sources[0][..., None, :]
        gap_y = target[1][..., :, None] - sources[1][..., None, :]
        gap_z = target[2][..., :, None] - sources[2][..., None, :]
        strength = jnp.where(itself, 0.0, kernel(gap_x, gap_y, gap_z))
        return lax.optimization_barrier(jnp.sum(strength * sources[3][..., None, :], axis=-1)).reshape(width_y, LZ * PPL)
    return lax.map(one_column, jnp.arange(count_x))

def box_surface(unit_cube, height, column_x, group_y):
    span_y = CYL * 2 ** height
    centre = [(column_x + 0.5) * CXL, (group_y + 0.5) * span_y, 0.5 * LZ]
    halves = [0.5 * CXL, 0.5 * span_y, 0.5 * LZ]
    return jnp.stack([centre[axis_id] + SURFACE_REACH * halves[axis_id] * unit_cube[axis_id] for axis_id in range(3)])

def check_terms(coords, weights, surfaces):
    per_level = []
    for surface in surfaces:
        strength = kernel(surface[0][:, None] - coords[0][None, :], surface[1][:, None] - coords[1][None, :], surface[2][:, None] - coords[2][None, :])
        per_level.append(jnp.dot(strength, weights, precision=PRECISE))
    return jnp.stack(per_level)

def far_values(coords, surface, panel_now):
    strength = kernel(coords[0][:, None] - surface[0][None, :], coords[1][:, None] - surface[1][None, :], coords[2][:, None] - surface[2][None, :])
    return jnp.dot(strength, panel_now, precision=PRECISE)

def box_multipoles(checks, height, up_ops):
    count_x, count_y = (checks.shape[0], checks.shape[1])
    summed = checks[:, :, height - 1, :].reshape(count_x, count_y >> height, 2 ** height, checks.shape[3]).sum(axis=2)
    return jnp.dot(summed.reshape(-1, checks.shape[3]), up_ops[height - 1], precision=PRECISE)

def reference(positions, charges, counts, up_ops, m2l_ops, down_ops, box_lists):
    unit_cube = surface_points(P_ORD)
    weights, occupied = live_charges(charges, counts)
    local_rows = jnp.concatenate([positions, weights[None]], axis=0)
    padded = jnp.pad(local_rows, ((0, 0), (1, 1), (1, 1), (0, 0)))
    near_part = near_field(padded, NYL)
    coords = absolute(positions, jnp.float32(0.0), jnp.float32(0.0))
    slots = LZ * PPL
    block_coords = coords.reshape(3, N_GX, CXL, N_GY, CYL, slots).transpose(1, 3, 0, 2, 4, 5).reshape(N_GX * N_GY, 3, CXL * CYL * slots)
    block_weights = weights.reshape(N_GX, CXL, N_GY, CYL, slots).transpose(0, 2, 1, 3, 4).reshape(N_GX * N_GY, CXL * CYL * slots)
    block_index = jnp.arange(N_GX * N_GY, dtype=jnp.int32)

    def block_surfaces(place_index):
        column_x = (place_index // N_GY).astype(jnp.float32)
        row_y = place_index % N_GY
        return [box_surface(unit_cube, height, column_x, (row_y >> height).astype(jnp.float32)) for height in range(1, LEV + 1)]

    def block_checks(inputs):
        coords_here, weights_here, place_index = inputs
        return check_terms(coords_here, weights_here, block_surfaces(place_index))
    checks = lax.map(block_checks, (block_coords, block_weights, block_index)).reshape(N_GX, N_GY, LEV, -1)
    multipoles = [box_multipoles(checks, height, up_ops) for height in range(1, LEV + 1)]
    panels = []
    offset = 0
    for height in range(1, LEV + 1):
        box_count = N_GX * (N_GY >> height)
        list_rows = box_lists[offset:offset + box_count]
        sources = multipoles[height - 1][list_rows]
        panels.append(jnp.einsum('bkf,kfe->be', sources, m2l_ops[height - 1], precision=PRECISE))
        offset = offset + box_count
    local_panel = panels[LEV - 1]
    for height in range(LEV - 1, 0, -1):
        across = N_GY >> height
        boxes = jnp.arange(N_GX * across, dtype=jnp.int32)
        column_x = boxes // across
        group_y = boxes % across
        parent = column_x * (across // 2) + group_y // 2
        above = local_panel[parent]
        lower = jnp.dot(above, down_ops[height - 1, 0], precision=PRECISE)
        upper = jnp.dot(above, down_ops[height - 1, 1], precision=PRECISE)
        local_panel = panels[height - 1] + jnp.where((group_y % 2 == 0)[:, None], lower, upper)
    first_box = block_index // N_GY * (N_GY // 2) + block_index % N_GY // 2
    block_panels = local_panel[first_box]

    def block_far(inputs):
        coords_here, panel_here, place_index = inputs
        return far_values(coords_here, block_surfaces(place_index)[0], panel_here)
    far_blocks = lax.map(block_far, (block_coords, block_panels, block_index))
    far_part = far_blocks.reshape(N_GX, N_GY, CXL, CYL, slots).transpose(0, 2, 1, 3, 4).reshape(NXL, NYL, slots)
    return jnp.where(occupied, near_part + far_part, 0.0)
```

```python
import jax
import jax.numpy as jnp
import numpy as np
from jax import lax
from jax.sharding import PartitionSpec as P

CXL = 8
CYL = 2
LZ = 8
PPL = 64
P_ORD = 8
LEV = 3


SOFTENING = 0.01
SURFACE_REACH = 1.05
PRECISE = lax.Precision.HIGHEST


def extended(cells, sides, width):
    for axis, dim in sides:
        count = lax.axis_size(axis)
        ends = count - 1
        head = lax.slice_in_dim(cells, 0, width, axis=dim)
        tail = lax.slice_in_dim(cells, cells.shape[dim] - width, cells.shape[dim], axis=dim)
        cells = jnp.concatenate(
            [
                lax.ppermute(tail, axis, [(i, (i + 1) % count) for i in range(ends)]),
                cells,
                lax.ppermute(head, axis, [((i + 1) % count, i) for i in range(ends)]),
            ],
            axis=dim,
        )
    return cells


def surface_points(order):
    lattice = np.linspace(-1.0, 1.0, order)
    points_list = []
    for first in range(order):
        for second in range(order):
            for third in range(order):
                if first in (0, order - 1) or second in (0, order - 1) or third in (0, order - 1):
                    points_list.append((lattice[first], lattice[second], lattice[third]))
    return jnp.asarray(np.array(points_list).T, dtype=jnp.float32)


def kernel(gap_x, gap_y, gap_z):
    return lax.rsqrt(gap_x * gap_x + gap_y * gap_y + gap_z * gap_z + SOFTENING)


def live_charges(charges, counts):
    size_x, size_y = (counts.shape[0], counts.shape[1])
    filled = jnp.broadcast_to(counts[..., None], (size_x, size_y, LZ, PPL)).reshape(
        size_x, size_y, LZ * PPL
    )
    within = jnp.arange(LZ * PPL, dtype=jnp.int32) % PPL
    occupied = within[None, None, :] < filled
    return (jnp.where(occupied, charges, 0.0), occupied)


def absolute(positions, anchor_x, anchor_y):
    size_x, size_y, slots = (positions.shape[1], positions.shape[2], positions.shape[3])
    along_x = anchor_x + jnp.arange(size_x).astype(jnp.float32)
    along_y = anchor_y + jnp.arange(size_y).astype(jnp.float32)
    along_z = (jnp.arange(slots) // PPL).astype(jnp.float32)
    return jnp.stack(
        [
            positions[0] + along_x[:, None, None],
            positions[1] + along_y[None, :, None],
            positions[2] + along_z[None, None, :],
        ]
    )


def near_field(padded, width_y):
    count_x = padded.shape[1] - 2
    blocks = padded.reshape(4, count_x + 2, width_y + 2, LZ, PPL)
    blocks = jnp.pad(blocks, ((0, 0), (0, 0), (0, 0), (1, 1), (0, 0)))
    rows_in = jnp.arange(PPL)[:, None]
    cols_in = jnp.arange(27 * PPL)[None, :]
    itself = cols_in == rows_in + 13 * PPL

    def one_column(column):
        window = lax.dynamic_slice_in_dim(blocks, column, 3, axis=1)
        target = window[:, 1, 1:-1, 1:-1, :]
        pieces = []
        for shift_x in range(3):
            for shift_y in range(3):
                for shift_z in range(3):
                    source = window[
                        :, shift_x, shift_y : shift_y + width_y, shift_z : shift_z + LZ, :
                    ]
                    pieces.append(
                        jnp.stack(
                            [
                                source[0] + (shift_x - 1.0),
                                source[1] + (shift_y - 1.0),
                                source[2] + (shift_z - 1.0),
                                source[3],
                            ]
                        )
                    )
        sources = jnp.concatenate(pieces, axis=-1)
        gap_x = target[0][..., :, None] - sources[0][..., None, :]
        gap_y = target[1][..., :, None] - sources[1][..., None, :]
        gap_z = target[2][..., :, None] - sources[2][..., None, :]
        strength = jnp.where(itself, 0.0, kernel(gap_x, gap_y, gap_z))
        return jnp.sum(strength * sources[3][..., None, :], axis=-1).reshape(width_y, LZ * PPL)

    return lax.map(one_column, jnp.arange(count_x))


def box_surface(unit_cube, height, column_x, group_y):
    span_y = CYL * 2**height
    centre = [(column_x + 0.5) * CXL, (group_y + 0.5) * span_y, 0.5 * LZ]
    halves = [0.5 * CXL, 0.5 * span_y, 0.5 * LZ]
    return jnp.stack(
        [
            centre[axis_id] + SURFACE_REACH * halves[axis_id] * unit_cube[axis_id]
            for axis_id in range(3)
        ]
    )


def check_terms(coords, weights, surfaces):
    per_level = []
    for surface in surfaces:
        strength = kernel(
            surface[0][:, None] - coords[0][None, :],
            surface[1][:, None] - coords[1][None, :],
            surface[2][:, None] - coords[2][None, :],
        )
        per_level.append(jnp.dot(strength, weights, precision=PRECISE))
    return jnp.stack(per_level)


def far_values(coords, surface, panel_now):
    strength = kernel(
        coords[0][:, None] - surface[0][None, :],
        coords[1][:, None] - surface[1][None, :],
        coords[2][:, None] - surface[2][None, :],
    )
    return jnp.dot(strength, panel_now, precision=PRECISE)


def box_multipoles(checks, height, up_ops):
    count_x, count_y = (checks.shape[0], checks.shape[1])
    summed = (
        checks[:, :, height - 1, :]
        .reshape(count_x, count_y >> height, 2**height, checks.shape[3])
        .sum(axis=2)
    )
    return jnp.dot(summed.reshape(-1, checks.shape[3]), up_ops[height - 1], precision=PRECISE)


def per_device(positions, charges, counts, up_ops, m2l_ops, down_ops, box_lists):
    unit_cube = surface_points(P_ORD)
    width_x, width_y = (positions.shape[1], positions.shape[2])
    index_x = lax.axis_index("gx")
    index_y = lax.axis_index("gy")
    devices_x = lax.axis_size("gx")
    devices_y = lax.axis_size("gy")
    weights, occupied = live_charges(charges, counts)
    local_rows = jnp.concatenate([positions, weights[None]], axis=0)
    padded = extended(local_rows, (("gx", 1), ("gy", 2)), 1)
    near_part = near_field(padded, width_y)
    coords = absolute(
        positions, (index_x * width_x).astype(jnp.float32), (index_y * width_y).astype(jnp.float32)
    )
    flat_coords = coords.reshape(3, -1)
    flat_weights = weights.reshape(-1)
    column_x = index_x.astype(jnp.float32)
    surfaces = [
        box_surface(unit_cube, height, column_x, (index_y >> height).astype(jnp.float32))
        for height in range(1, LEV + 1)
    ]
    own_checks = check_terms(flat_coords, flat_weights, surfaces)
    rank_count = devices_x * devices_y
    width = own_checks.shape[0] * own_checks.shape[1]
    flat_checks = jnp.pad(own_checks.reshape(1, 1, width), ((0, 0), (0, 0), (0, -width % 128)))
    copies = jnp.broadcast_to(flat_checks, (rank_count, 1, flat_checks.shape[2]))
    gathered = lax.all_to_all(copies, ("gx", "gy"), 0, 0, tiled=True)
    checks = gathered[:, 0, :width].reshape(
        devices_x, devices_y, own_checks.shape[0], own_checks.shape[1]
    )
    multipoles = [box_multipoles(checks, height, up_ops) for height in range(1, LEV + 1)]
    panel_above = None
    for height in range(LEV, 0, -1):
        across = devices_y >> height
        group_y = index_y >> height
        box_id = index_x * across + group_y
        offset = devices_x * (devices_y - (devices_y >> height - 1))
        list_row = lax.dynamic_slice_in_dim(box_lists, offset + box_id, 1, 0)[0]
        chooser = (
            list_row[:, None] == jnp.arange(devices_x * across, dtype=jnp.int32)[None, :]
        ).astype(jnp.float32)
        sources = jnp.dot(chooser, multipoles[height - 1], precision=PRECISE)
        panel_now = jnp.einsum("kf,kfe->e", sources, m2l_ops[height - 1], precision=PRECISE)
        if panel_above is not None:
            side_bit = group_y % 2
            matrix = jnp.where(side_bit == 0, down_ops[height - 1, 0], down_ops[height - 1, 1])
            panel_now = panel_now + jnp.dot(panel_above, matrix, precision=PRECISE)
        panel_above = panel_now
    far_part = far_values(flat_coords, surfaces[0], panel_above).reshape(weights.shape)
    return jnp.where(occupied, near_part + far_part, 0.0)


def solution(mesh):
    return jax.shard_map(
        per_device,
        mesh=mesh,
        in_specs=(
            P(None, "gx", "gy", None),
            P("gx", "gy", None),
            P("gx", "gy", None),
            P(),
            P(),
            P(),
            P(),
        ),
        out_specs=P("gx", "gy", None),
        check_vma=False,
    )
```

```python
import functools
import jax
import jax.numpy as jnp
import numpy as np
from jax import lax
from jax.experimental import pallas as pl
from jax.experimental.pallas import tpu as pltpu
from jax.sharding import PartitionSpec as P

CXL = 8
CYL = 2
LZ = 8
PPL = 64
P_ORD = 8
K = 8
LEV = 3
NE = 296
SLOTS = LZ * PPL
LANES = 128
ROWS = CXL * CYL * SLOTS // LANES
SOFTENING = 0.01
SURFACE_REACH = 1.05
PRECISE = lax.Precision.HIGHEST
LATTICE = np.linspace(-1.0, 1.0, P_ORD)
CHUNKS = ((0, 128), (128, 256), (256, NE))
INNER = range(1, P_ORD - 1)
ENDS = (0, P_ORD - 1)
A_TILES = [(a, b) for a in ENDS for b in range(P_ORD)]
B_TILES = [(a, b) for b in ENDS for a in INNER]
C_TILES = [(b, c) for c in ENDS for b in INNER]


def first_row(a, b):
    if a == 0:
        return 8 * b
    if a == P_ORD - 1:
        return 232 + 8 * b
    return 64 + 28 * (a - 1) + (0 if b == 0 else 20)


def strided_rows(b, c):
    return pl.ds(64 + 8 + 2 * (b - 1) + (1 if c else 0), P_ORD - 2, stride=28)


def wide(row):
    return jnp.broadcast_to(row, (8, LANES))


def lattice_x(a):
    return float(0.5 * CXL + SURFACE_REACH * 0.5 * CXL * LATTICE[a])


def lattice_z(c):
    return float(0.5 * LZ + SURFACE_REACH * 0.5 * LZ * LATTICE[c])


def along_sublanes(half):
    steps = lax.broadcasted_iota(jnp.int32, (8, LANES), 0).astype(jnp.float32)
    return half - SURFACE_REACH * half + steps * (SURFACE_REACH * half * 2.0 / (P_ORD - 1))


def square(value):
    return value * value


def a_squares(x8, z8, y_parts):
    along_z = square(along_sublanes(0.5 * LZ) - z8) + SOFTENING
    for a in ENDS:
        base = square(lattice_x(a) - x8) + along_z
        for b in range(P_ORD):
            yield base + y_parts[b]


def bc_squares(x8, z8, y_parts):
    along_z = square(along_sublanes(0.5 * LZ) - z8) + SOFTENING
    bases = [square(lattice_x(a) - x8) + along_z for a in INNER]
    for b in ENDS:
        for base in bases:
            yield base + y_parts[b]
    along_x = square(along_sublanes(0.5 * CXL) - x8) + SOFTENING
    for c in ENDS:
        base = along_x + square(lattice_z(c) - z8)
        for b in INNER:
            yield base + y_parts[b]


def row_of(p_ref, r):
    return [wide(p_ref[c, pl.ds(r, 1), :]) for c in range(4)]


def send_kernel(
    span_x, span_y, meta_ref, sy_ref, p_ref, up_hbm, m2l_hbm, down_hbm, out_ref,
    up_ref, m2l_ref, down_ref, check_ref, row_ref, column_ref, panel_ref, sems,
):
    copies = [pltpu.make_async_copy(up_hbm, up_ref, sems.at[0])]
    copies += [
        pltpu.make_async_copy(m2l_hbm.at[h], m2l_ref.at[h], sems.at[1 + h]) for h in range(LEV)
    ]
    copies.append(pltpu.make_async_copy(down_hbm, down_ref, sems.at[1 + LEV]))
    for copy in copies:
        copy.start()
    row_ref[...] = jnp.zeros((8, 384), jnp.float32)

    for h in range(LEV):
        ys = [sy_ref[8 * h + b] for b in range(P_ORD)]
        for squares, tiles in ((a_squares, A_TILES), (bc_squares, B_TILES + C_TILES)):

            def gather(r, sums):
                x8, y8, z8, w8 = row_of(p_ref, r)
                y_parts = [square(ys[b] - y8) for b in range(P_ORD)]
                return [
                    total + w8 * lax.rsqrt(d2)
                    for total, d2 in zip(sums, squares(x8, z8, y_parts))
                ]

            sums = lax.fori_loop(
                0, ROWS, gather, [jnp.zeros((8, LANES), jnp.float32) for _ in tiles], unroll=2
            )
            for n, (total, tile) in enumerate(zip(sums, tiles)):
                filled = jnp.broadcast_to(jnp.sum(total, axis=1, keepdims=True), (8, LANES))
                if squares is bc_squares and n >= len(B_TILES):
                    check_ref[h, strided_rows(*tile), :] = filled[1:7]
                else:
                    check_ref[h, pl.ds(first_row(*tile), 8), :] = filled

    copies[0].wait()
    for h in range(LEV):
        for low, high in CHUNKS:
            total = jnp.zeros((8, high - low), jnp.float32)
            for i in range(0, NE, 8):
                total += check_ref[h, i : i + 8, : high - low] * up_ref[h, i : i + 8, low:high]
            row_ref[h : h + 1, low:high] = jnp.sum(total, axis=0, keepdims=True)
    flipped = jnp.transpose(row_ref[...])
    for h in range(LEV):
        column_ref[h] = jnp.broadcast_to(flipped[:NE, h : h + 1], (NE, LANES))

    for h in range(LEV):
        copies[1 + h].wait()

        def translate(k, carry):
            for low, high in CHUNKS:
                total = jnp.zeros((8, high - low), jnp.float32)
                for i in range(0, NE, 8):
                    total += (
                        column_ref[h, i : i + 8, : high - low]
                        * m2l_ref[h, k, i : i + 8, low:high]
                    )
                panel_ref[h, k, :, low:high] = total
            return carry

        lax.fori_loop(0, K, translate, 0)

    copies[1 + LEV].wait()
    panels = [jnp.sum(panel_ref[h], axis=1) for h in range(LEV)]
    top = panels[2]
    middle = jnp.concatenate(
        [panels[1]]
        + [
            jnp.dot(top, down_ref[1, side], precision=PRECISE, preferred_element_type=jnp.float32)
            for side in range(2)
        ],
        axis=0,
    )
    lower = [
        jnp.dot(middle, down_ref[0, side], precision=PRECISE, preferred_element_type=jnp.float32)
        for side in range(2)
    ]
    out_ref[...] = jnp.zeros(out_ref.shape, jnp.float32)
    sub = lax.broadcasted_iota(jnp.int32, (8, NE), 0)
    index_x = meta_ref[0]
    index_y = meta_ref[1]

    def spread(row):
        return jnp.broadcast_to(row, (8, NE))

    for h in range(1, LEV + 1):
        across = span_y >> h
        bits = across.bit_length() - 1
        own_box = (index_x << bits) + (index_y >> h)
        for k in range(K):
            box = (own_box - meta_ref[2 + (h - 1) * K + k]) & (span_x * across - 1)
            place_y = (box & (across - 1)) << h
            tile = (box >> bits) * (span_y // 8) + (place_y >> 3)
            inside = place_y & 7
            if h == 1:
                value = spread(panels[0][k : k + 1])
            else:
                first = 0 if h == 2 else 8
                value = jnp.where(
                    (sub // 2) % 2 == 0,
                    spread(lower[0][first + k : first + k + 1]),
                    spread(lower[1][first + k : first + k + 1]),
                )
                if h == 3:
                    upper = jnp.where(
                        (sub // 2) % 2 == 0,
                        spread(lower[0][16 + k : 17 + k]),
                        spread(lower[1][16 + k : 17 + k]),
                    )
                    value = jnp.where(sub < 4, value, upper)
            if h < 3:
                value = jnp.where((sub >= inside) & (sub < inside + 2**h), value, 0.0)
            out_ref[tile] = out_ref[tile] + value


def send_panels(meta, sy, points, up_ops, m2l_ops, down_ops, span_x, span_y):
    return pl.pallas_call(
        functools.partial(send_kernel, span_x, span_y),
        out_shape=jax.ShapeDtypeStruct((span_x * span_y // 8, 8, NE), jnp.float32),
        in_specs=[
            pl.BlockSpec(memory_space=pltpu.SMEM),
            pl.BlockSpec(memory_space=pltpu.SMEM),
            pl.BlockSpec(memory_space=pltpu.VMEM),
            pl.BlockSpec(memory_space=pl.ANY),
            pl.BlockSpec(memory_space=pl.ANY),
            pl.BlockSpec(memory_space=pl.ANY),
        ],
        out_specs=pl.BlockSpec(memory_space=pltpu.VMEM),
        scratch_shapes=[
            pltpu.VMEM((LEV, NE, NE), jnp.float32),
            pltpu.VMEM((LEV, K, NE, NE), jnp.float32),
            pltpu.VMEM((LEV - 1, 2, NE, NE), jnp.float32),
            pltpu.VMEM((LEV, NE, LANES), jnp.float32),
            pltpu.VMEM((8, 384), jnp.float32),
            pltpu.VMEM((LEV, NE, LANES), jnp.float32),
            pltpu.VMEM((LEV, K, 8, NE), jnp.float32),
            pltpu.SemaphoreType.DMA((LEV + 2,)),
        ],
        compiler_params=pltpu.CompilerParams(vmem_limit_bytes=40 * 2**20),
        name="send_panels",
    )(meta, sy, points, up_ops, m2l_ops, down_ops)


def far_kernel(
    sy_ref, p_ref, held_ref, low_ref, high_ref, parts_ref, out_ref, row_ref, column_ref, tile_ref,
    near_ref,
):
    row_ref[...] = jnp.zeros((8, 384), jnp.float32)
    near_ref[: ROWS // 2, :] = low_ref[...]
    near_ref[ROWS // 2 :, :] = high_ref[...]
    row_ref[0:1, :NE] = jnp.sum(parts_ref[...], axis=0, keepdims=True)
    flipped = jnp.transpose(row_ref[...])
    column_ref[...] = jnp.broadcast_to(flipped[:NE, 0:1], (NE, LANES))
    for n, tile in enumerate(A_TILES + B_TILES):
        tile_ref[n] = column_ref[pl.ds(first_row(*tile), 8), :]
    for n, tile in enumerate(C_TILES):
        n += len(A_TILES + B_TILES)
        tile_ref[n] = jnp.zeros((8, LANES), jnp.float32)
        tile_ref[n, 1:7, :] = column_ref[strided_rows(*tile), :]
    ys = [sy_ref[b] for b in range(P_ORD)]

    def spread(r, carry):
        x8, y8, z8, w8 = row_of(p_ref, r)
        y_parts = [square(ys[b] - y8) for b in range(P_ORD)]
        totals = [jnp.zeros((8, LANES), jnp.float32) for _ in range(4)]
        n = 0
        for squares in (a_squares, bc_squares):
            for d2 in squares(x8, z8, y_parts):
                totals[n % 4] += tile_ref[n] * lax.rsqrt(d2)
                n += 1
        far = jnp.sum(totals[0] + totals[1] + (totals[2] + totals[3]), axis=0, keepdims=True)
        here = pl.ds(r, 1)
        value = near_ref[here, :] + far
        out_ref[here, :] = jnp.where(held_ref[here, :] > 0, value, 0.0)
        return carry

    lax.fori_loop(0, ROWS, spread, 0, unroll=2)


def far_and_sum(sy, points, held, low, high, parts):
    return pl.pallas_call(
        far_kernel,
        out_shape=jax.ShapeDtypeStruct((ROWS, LANES), jnp.float32),
        in_specs=[pl.BlockSpec(memory_space=pltpu.SMEM)]
        + [pl.BlockSpec(memory_space=pltpu.VMEM)] * 5,
        out_specs=pl.BlockSpec(memory_space=pltpu.VMEM),
        scratch_shapes=[
            pltpu.VMEM((8, 384), jnp.float32),
            pltpu.VMEM((NE, LANES), jnp.float32),
            pltpu.VMEM((40, 8, LANES), jnp.float32),
            pltpu.VMEM((ROWS, LANES), jnp.float32),
        ],
        compiler_params=pltpu.CompilerParams(vmem_limit_bytes=16 * 2**20),
        name="far_and_sum",
    )(sy, points, held, low, high, parts)


PAD_Z = LZ + 2
STEP = 4


def near_kernel(first_x, count_x, fill_ref, source_ref, column_ref, out_ref, sum_ref):
    lanes = lax.broadcasted_iota(jnp.int32, (8, LANES), 1)
    lower_half = lanes < PPL
    ones = jnp.ones((8, LANES), jnp.bfloat16)
    own = lax.rsqrt(jnp.full((1, LANES), SOFTENING, jnp.float32))

    def one_leaf_pair(leaf, carry):
        x = leaf // LZ
        z = leaf % LZ
        held = jnp.maximum(
            fill_ref[(first_x + x) * 2 * LZ + z], fill_ref[((first_x + x) * 2 + 1) * LZ + z]
        )

        def add_tiles(step, inner):
            targets = []
            for u in range(STEP):
                start = pl.multiple_of(8 * (STEP * step + u), 8)
                block = column_ref[first_x + x, pl.ds(start, 8), :]

                def pick(c, y):
                    lane = jnp.full((8, LANES), (c * 2 + y) * LZ, jnp.int32) + z
                    return jnp.take_along_axis(block, lane, axis=1)

                low = [pick(c, 0) for c in range(3)]
                high = [pick(c, 1) for c in range(3)]
                mixed = [jnp.where(lower_half, l, h) for l, h in zip(low, high)]
                targets.append((low, high, mixed))
            sums = [[None] * 3 for _ in range(STEP)]
            for shift_x in range(3):
                for shift_z in range(3):
                    row = (first_x + x + shift_x) * PAD_Z + z + shift_z
                    for side in range(2):
                        source = [
                            wide(source_ref[4 * side + c, pl.ds(row, 1), :]) for c in range(4)
                        ]
                        for u in range(STEP):
                            for n in (0, 1) if side == 0 else (2,):
                                tx, ty, tz = targets[u][n]
                                d2 = square(tx - source[0]) + SOFTENING
                                d2 += square(ty - source[1])
                                d2 += square(tz - source[2])
                                value = source[3] * lax.rsqrt(d2)
                                old = sums[u][n]
                                sums[u][n] = value if old is None else old + value
            for u in range(STEP):
                low, high, mixed = sums[u]
                start = pl.multiple_of(8 * (STEP * step + u), 8)
                sum_ref[leaf, pl.ds(start, 8), :] = low + jnp.where(lower_half, mixed, 0.0)
                sum_ref[leaf, pl.ds(PPL + start, 8), :] = high + jnp.where(lower_half, 0.0, mixed)
            return inner

        lax.fori_loop(0, (held + 8 * STEP - 1) // (8 * STEP), add_tiles, 0)
        return carry

    lax.fori_loop(0, count_x * LZ, one_leaf_pair, 0)

    def finish(group, carry):
        rows = []
        for n in range(8):
            rest = sum_ref[8 * group + n]
            total = None
            for _ in range(3):
                part = rest.astype(jnp.bfloat16)
                rest = rest - part.astype(jnp.float32)
                term = lax.dot_general(
                    ones, part, (((1,), (1,)), ((), ())), preferred_element_type=jnp.float32
                )
                total = term if total is None else total + term
            own_row = (first_x + group + 1) * PAD_Z + n + 1
            rows.append(total[0:1] - source_ref[3, pl.ds(own_row, 1), :] * own)
        out_ref[pl.ds(pl.multiple_of(8 * group, 8), 8), :] = jnp.concatenate(rows, axis=0)
        return carry

    lax.fori_loop(0, count_x, finish, 0)


def near_sums(first_x, count_x, fill, sources, columns):
    return pl.pallas_call(
        functools.partial(near_kernel, first_x, count_x),
        out_shape=jax.ShapeDtypeStruct((count_x * LZ, LANES), jnp.float32),
        in_specs=[pl.BlockSpec(memory_space=pltpu.SMEM)]
        + [pl.BlockSpec(memory_space=pltpu.VMEM)] * 2,
        out_specs=pl.BlockSpec(memory_space=pltpu.VMEM),
        scratch_shapes=[pltpu.VMEM((count_x * LZ, LANES, LANES), jnp.float32)],
        compiler_params=pltpu.CompilerParams(vmem_limit_bytes=24 * 2**20),
        name="near_sums",
    )(fill, sources, columns)


def extended(cells, sides, width):
    for axis, dim in sides:
        count = lax.axis_size(axis)
        ends = count - 1
        head = lax.slice_in_dim(cells, 0, width, axis=dim)
        tail = lax.slice_in_dim(cells, cells.shape[dim] - width, cells.shape[dim], axis=dim)
        cells = jnp.concatenate(
            [
                lax.ppermute(tail, axis, [(i, (i + 1) % count) for i in range(ends)]),
                cells,
                lax.ppermute(head, axis, [((i + 1) % count, i) for i in range(ends)]),
            ],
            axis=dim,
        )
    return cells


def live_charges(charges, counts):
    size_x, size_y = (counts.shape[0], counts.shape[1])
    filled = jnp.broadcast_to(counts[..., None], (size_x, size_y, LZ, PPL)).reshape(
        size_x, size_y, SLOTS
    )
    within = jnp.arange(SLOTS, dtype=jnp.int32) % PPL
    occupied = within[None, None, :] < filled
    return (jnp.where(occupied, charges, 0.0), occupied)


def placed(rows, start_x, start_y):
    size_x, size_y = rows.shape[1:3]
    along_x = (start_x + jnp.arange(size_x)).astype(jnp.float32)
    along_y = (start_y + jnp.arange(size_y)).astype(jnp.float32)
    along_z = (jnp.arange(SLOTS) // PPL).astype(jnp.float32)
    return jnp.stack(
        [
            rows[0] + along_x[:, None, None],
            rows[1] + along_y[None, :, None],
            rows[2] + along_z[None, None, :],
            rows[3],
        ]
    )


def leaf_pairs(cells):
    lead, size_x = cells.shape[:2]
    split = cells.reshape(lead, size_x, 2, LZ, PPL).transpose(0, 1, 3, 2, 4)
    return split.reshape(lead, size_x, LZ, LANES)


def per_device(positions, charges, counts, up_ops, m2l_ops, down_ops, box_lists):
    index_x = lax.axis_index("gx")
    index_y = lax.axis_index("gy")
    devices_x = lax.axis_size("gx")
    devices_y = lax.axis_size("gy")
    weights, occupied = live_charges(charges, counts)
    local_rows = jnp.concatenate([positions, weights[None]], axis=0)
    padded = extended(local_rows, (("gx", 1), ("gy", 2)), 1)

    own = placed(local_rows, 0, 0)
    points = leaf_pairs(own).reshape(4, ROWS, LANES)
    held = leaf_pairs(occupied.astype(jnp.float32)[None]).reshape(ROWS, LANES)
    offsets = [devices_x * (devices_y - (devices_y >> h - 1)) for h in range(1, LEV + 1)]
    meta = jnp.concatenate([jnp.stack([index_x, index_y])] + [box_lists[o] for o in offsets])
    lattice = jnp.asarray(LATTICE, dtype=jnp.float32)
    sy = jnp.concatenate(
        [
            ((index_y >> h) * CYL * 2**h - index_y * CYL).astype(jnp.float32)
            + (0.5 * CYL * 2**h) * (1.0 + SURFACE_REACH * lattice)
            for h in range(1, LEV + 1)
        ]
    )
    sent = send_panels(meta, sy, points, up_ops, m2l_ops, down_ops, devices_x, devices_y)
    along_x = lax.all_to_all(
        sent.reshape(devices_x, devices_y, NE), "gx", split_axis=0, concat_axis=0, tiled=True
    )
    middle = jnp.sum(along_x, axis=0).reshape(devices_y, 1, NE)
    parts = lax.all_to_all(middle, "gy", split_axis=0, concat_axis=0, tiled=True)

    around = placed(padded, -1, -1)
    sources = jnp.concatenate(
        [leaf_pairs(around[:, :, 1:3]), leaf_pairs(jnp.stack([around[:, :, 0], around[:, :, 3]], 2))]
    )
    sources = jnp.pad(sources, ((0, 0), (0, 0), (1, 1), (0, 0)))
    sources = sources.reshape(8, (CXL + 2) * PAD_Z, LANES)
    columns = own[:3].reshape(3, CXL, CYL, LZ, PPL).transpose(1, 4, 0, 2, 3)
    columns = columns.reshape(CXL, PPL, 3 * CYL * LZ)
    columns = jnp.pad(columns, ((0, 0), (0, 0), (0, LANES - columns.shape[2])))
    fill = counts.reshape(-1)
    half = CXL // 2
    near = [near_sums(0, half, fill, sources, columns)]
    near.append(near_sums(half, half, fill, sources, columns))
    total = far_and_sum(sy, points, held, near[0], near[1], parts.reshape(devices_y, NE))
    total = total.reshape(CXL, LZ, CYL, PPL).transpose(0, 2, 1, 3)
    return total.reshape(CXL, CYL, SLOTS)


def solution(mesh):
    return jax.shard_map(
        per_device,
        mesh=mesh,
        in_specs=(
            P(None, "gx", "gy", None),
            P("gx", "gy", None),
            P("gx", "gy", None),
            P(),
            P(),
            P(),
            P(),
        ),
        out_specs=P("gx", "gy", None),
        check_vma=False,
    )
```

```python
import functools
import jax
import jax.numpy as jnp
import numpy as np
from jax import lax
from jax.experimental import pallas as pl
from jax.experimental.pallas import tpu as pltpu
from jax.sharding import PartitionSpec as P

CXL = 8
CYL = 2
LZ = 8
PPL = 64
P_ORD = 8
K = 8
LEV = 3
NE = 296
SLOTS = LZ * PPL
LANES = 128
ROWS = CXL * CYL * SLOTS // LANES
SOFTENING = 0.01
SURFACE_REACH = 1.05
PRECISE = lax.Precision.HIGHEST
LATTICE = np.linspace(-1.0, 1.0, P_ORD)
CHUNKS = ((0, 128), (128, 256), (256, NE))
INNER = range(1, P_ORD - 1)
ENDS = (0, P_ORD - 1)
A_TILES = [(a, b) for a in ENDS for b in range(P_ORD)]
B_TILES = [(a, b) for b in ENDS for a in INNER]
C_TILES = [(b, c) for c in ENDS for b in INNER]


def first_row(a, b):
    if a == 0:
        return 8 * b
    if a == P_ORD - 1:
        return 232 + 8 * b
    return 64 + 28 * (a - 1) + (0 if b == 0 else 20)


def strided_rows(b, c):
    return pl.ds(64 + 8 + 2 * (b - 1) + (1 if c else 0), P_ORD - 2, stride=28)


def wide(row):
    return jnp.broadcast_to(row, (8, LANES))


def lattice_x(a):
    return float(0.5 * CXL + SURFACE_REACH * 0.5 * CXL * LATTICE[a])


def lattice_z(c):
    return float(0.5 * LZ + SURFACE_REACH * 0.5 * LZ * LATTICE[c])


def along_sublanes(half):
    steps = lax.broadcasted_iota(jnp.int32, (8, LANES), 0).astype(jnp.float32)
    return half - SURFACE_REACH * half + steps * (SURFACE_REACH * half * 2.0 / (P_ORD - 1))


def square(value):
    return value * value


def a_squares(x8, z8, y_parts):
    along_z = square(along_sublanes(0.5 * LZ) - z8) + SOFTENING
    for a in ENDS:
        base = square(lattice_x(a) - x8) + along_z
        for b in range(P_ORD):
            yield base + y_parts[b]


def bc_squares(x8, z8, y_parts):
    along_z = square(along_sublanes(0.5 * LZ) - z8) + SOFTENING
    bases = [square(lattice_x(a) - x8) + along_z for a in INNER]
    for b in ENDS:
        for base in bases:
            yield base + y_parts[b]
    along_x = square(along_sublanes(0.5 * CXL) - x8) + SOFTENING
    for c in ENDS:
        base = along_x + square(lattice_z(c) - z8)
        for b in INNER:
            yield base + y_parts[b]


def row_of(p_ref, r):
    return [wide(p_ref[c, pl.ds(r, 1), :]) for c in range(4)]


def send_kernel(
    span_x, span_y, meta_ref, sy_ref, p_ref, up_hbm, m2l_hbm, down_hbm, out_ref,
    up_ref, m2l_ref, down_ref, check_ref, row_ref, column_ref, panel_ref, sems,
):
    copies = [pltpu.make_async_copy(up_hbm, up_ref, sems.at[0])]
    copies += [
        pltpu.make_async_copy(m2l_hbm.at[h], m2l_ref.at[h], sems.at[1 + h]) for h in range(LEV)
    ]
    copies.append(pltpu.make_async_copy(down_hbm, down_ref, sems.at[1 + LEV]))
    for copy in copies:
        copy.start()
    row_ref[...] = jnp.zeros((8, 384), jnp.float32)

    for h in range(LEV):
        ys = [sy_ref[8 * h + b] for b in range(P_ORD)]
        for squares, tiles in ((a_squares, A_TILES), (bc_squares, B_TILES + C_TILES)):

            def gather(r, sums):
                x8, y8, z8, w8 = row_of(p_ref, r)
                y_parts = [square(ys[b] - y8) for b in range(P_ORD)]
                return [
                    total + w8 * lax.rsqrt(d2)
                    for total, d2 in zip(sums, squares(x8, z8, y_parts))
                ]

            sums = lax.fori_loop(
                0, ROWS, gather, [jnp.zeros((8, LANES), jnp.float32) for _ in tiles], unroll=2
            )
            for n, (total, tile) in enumerate(zip(sums, tiles)):
                filled = jnp.broadcast_to(jnp.sum(total, axis=1, keepdims=True), (8, LANES))
                if squares is bc_squares and n >= len(B_TILES):
                    check_ref[h, strided_rows(*tile), :] = filled[1:7]
                else:
                    check_ref[h, pl.ds(first_row(*tile), 8), :] = filled

    copies[0].wait()
    for h in range(LEV):
        for low, high in CHUNKS:
            total = jnp.zeros((8, high - low), jnp.float32)
            for i in range(0, NE, 8):
                total += check_ref[h, i : i + 8, : high - low] * up_ref[h, i : i + 8, low:high]
            row_ref[h : h + 1, low:high] = jnp.sum(total, axis=0, keepdims=True)
    flipped = jnp.transpose(row_ref[...])
    for h in range(LEV):
        column_ref[h] = jnp.broadcast_to(flipped[:NE, h : h + 1], (NE, LANES))

    for h in range(LEV):
        copies[1 + h].wait()

        def translate(k, carry):
            for low, high in CHUNKS:
                total = jnp.zeros((8, high - low), jnp.float32)
                for i in range(0, NE, 8):
                    total += (
                        column_ref[h, i : i + 8, : high - low]
                        * m2l_ref[h, k, i : i + 8, low:high]
                    )
                panel_ref[h, k, :, low:high] = total
            return carry

        lax.fori_loop(0, K, translate, 0)

    copies[1 + LEV].wait()
    panels = [jnp.sum(panel_ref[h], axis=1) for h in range(LEV)]
    top = panels[2]
    middle = jnp.concatenate(
        [panels[1]]
        + [
            jnp.dot(top, down_ref[1, side], precision=PRECISE, preferred_element_type=jnp.float32)
            for side in range(2)
        ],
        axis=0,
    )
    lower = [
        jnp.dot(middle, down_ref[0, side], precision=PRECISE, preferred_element_type=jnp.float32)
        for side in range(2)
    ]
    out_ref[...] = jnp.zeros(out_ref.shape, jnp.float32)
    index_x = meta_ref[0]
    index_y = meta_ref[1]
    for h in range(1, LEV + 1):
        across = span_y >> h
        bits = across.bit_length() - 1
        own_box = (index_x << bits) + (index_y >> h)
        for k in range(K):
            box = (own_box - meta_ref[2 + (h - 1) * K + k]) & (span_x * across - 1)
            first = (box >> bits) * span_y + ((box & (across - 1)) << h)
            for j in range(2**h):
                if h == 1:
                    value = panels[0][k : k + 1]
                else:
                    start = 8 * (h - 2 + j // 4) + k
                    value = lower[j // 2 % 2][start : start + 1]
                out_ref[first + j] += value


def send_panels(meta, sy, points, up_ops, m2l_ops, down_ops, span_x, span_y):
    return pl.pallas_call(
        functools.partial(send_kernel, span_x, span_y),
        out_shape=jax.ShapeDtypeStruct((span_x * span_y, 1, NE), jnp.float32),
        in_specs=[
            pl.BlockSpec(memory_space=pltpu.SMEM),
            pl.BlockSpec(memory_space=pltpu.SMEM),
            pl.BlockSpec(memory_space=pltpu.VMEM),
            pl.BlockSpec(memory_space=pltpu.HBM),
            pl.BlockSpec(memory_space=pltpu.HBM),
            pl.BlockSpec(memory_space=pltpu.HBM),
        ],
        out_specs=pl.BlockSpec(memory_space=pltpu.VMEM),
        scratch_shapes=[
            pltpu.VMEM((LEV, NE, NE), jnp.float32),
            pltpu.VMEM((LEV, K, NE, NE), jnp.float32),
            pltpu.VMEM((LEV - 1, 2, NE, NE), jnp.float32),
            pltpu.VMEM((LEV, NE, LANES), jnp.float32),
            pltpu.VMEM((8, 384), jnp.float32),
            pltpu.VMEM((LEV, NE, LANES), jnp.float32),
            pltpu.VMEM((LEV, K, 8, NE), jnp.float32),
            pltpu.SemaphoreType.DMA((LEV + 2,)),
        ],
        compiler_params=pltpu.CompilerParams(vmem_limit_bytes=18 * 2**20),
        name="send_panels",
    )(meta, sy, points, up_ops, m2l_ops, down_ops)


def far_kernel(
    sy_ref, p_ref, held_ref, near_ref, parts_ref, out_ref, row_ref, column_ref, tile_ref,
):
    row_ref[...] = jnp.zeros((8, 384), jnp.float32)
    row_ref[0:1, :NE] = jnp.sum(parts_ref[...], axis=0)
    flipped = jnp.transpose(row_ref[...])
    column_ref[...] = jnp.broadcast_to(flipped[:NE, 0:1], (NE, LANES))
    for n, tile in enumerate(A_TILES + B_TILES):
        tile_ref[n] = column_ref[pl.ds(first_row(*tile), 8), :]
    for n, tile in enumerate(C_TILES):
        n += len(A_TILES + B_TILES)
        tile_ref[n] = jnp.zeros((8, LANES), jnp.float32)
        tile_ref[n, 1:7, :] = column_ref[strided_rows(*tile), :]
    ys = [sy_ref[b] for b in range(P_ORD)]

    def spread(r, carry):
        x8, y8, z8, w8 = row_of(p_ref, r)
        y_parts = [square(ys[b] - y8) for b in range(P_ORD)]
        totals = [jnp.zeros((8, LANES), jnp.float32) for _ in range(4)]
        n = 0
        for squares in (a_squares, bc_squares):
            for d2 in squares(x8, z8, y_parts):
                totals[n % 4] += tile_ref[n] * lax.rsqrt(d2)
                n += 1
        far = jnp.sum(totals[0] + totals[1] + (totals[2] + totals[3]), axis=0, keepdims=True)
        here = pl.ds(r, 1)
        value = near_ref[here, :] + far
        out_ref[here, :] = jnp.where(held_ref[here, :] > 0, value, 0.0)
        return carry

    lax.fori_loop(0, ROWS, spread, 0, unroll=2)


def far_and_sum(sy, points, held, near, parts):
    return pl.pallas_call(
        far_kernel,
        out_shape=jax.ShapeDtypeStruct((ROWS, LANES), jnp.float32),
        in_specs=[pl.BlockSpec(memory_space=pltpu.SMEM)]
        + [pl.BlockSpec(memory_space=pltpu.VMEM)] * 4,
        out_specs=pl.BlockSpec(memory_space=pltpu.VMEM),
        scratch_shapes=[
            pltpu.VMEM((8, 384), jnp.float32),
            pltpu.VMEM((NE, LANES), jnp.float32),
            pltpu.VMEM((40, 8, LANES), jnp.float32),
        ],
        compiler_params=pltpu.CompilerParams(vmem_limit_bytes=4 * 2**20),
        name="far_and_sum",
    )(sy, points, held, near, parts)


PAD_Z = LZ + 2
PLANES = 5
STEP = 2
TILES = PPL // 8
LEAVES = CXL * LZ
COLUMNS = 3 * CYL * LZ


def choices():
    chosen = np.zeros((LZ, 2 * LANES, 3 * CYL * LANES), np.float32)
    for z in range(LZ):
        for n in range(3 * CYL):
            for part in range(3):
                chosen[z, part * COLUMNS + n * LZ + z, n * LANES : (n + 1) * LANES] = 1.0
    return jnp.asarray(chosen, dtype=jnp.bfloat16)


def near_kernel(fill_ref, source_ref, column_ref, choice_ref, out_ref, sum_ref, place_ref):
    lanes = lax.broadcasted_iota(jnp.int32, (8, LANES), 1)
    slots = lax.broadcasted_iota(jnp.int32, (8, LANES), 0)
    lower_half = lanes < PPL
    rest = column_ref[...]
    high_part = rest.astype(jnp.bfloat16)
    rest = rest - high_part.astype(jnp.float32)
    middle_part = rest.astype(jnp.bfloat16)
    low_part = (rest - middle_part.astype(jnp.float32)).astype(jnp.bfloat16)
    column = lax.broadcasted_iota(jnp.int32, rest.shape, 1)
    split = jnp.where(
        column < COLUMNS,
        high_part.astype(jnp.float32),
        jnp.where(
            column < 2 * COLUMNS, middle_part.astype(jnp.float32), low_part.astype(jnp.float32)
        ),
    ).astype(jnp.bfloat16)
    for z in range(LZ):
        place_ref[z] = jnp.dot(split, choice_ref[z], preferred_element_type=jnp.float32)

    def add_tiles(leaf, step):
        x = leaf // LZ
        z = leaf % LZ
        targets = []
        for u in range(STEP):
            start = pl.multiple_of(x * PPL + 8 * (STEP * step + u), 8)
            low, high = [
                [
                    place_ref[z, pl.ds(start, 8), LANES * (2 * c + y) : LANES * (2 * c + y + 1)]
                    for c in range(3)
                ]
                for y in range(2)
            ]
            for place in (low, high):
                place.append(square(place[0]) + square(place[1]) + square(place[2]))
            mixed = [jnp.where(lower_half, l, h) for l, h in zip(low, high)]
            targets.append((low, high, mixed))
        sums = [[None] * 3 for _ in range(STEP)]
        for shift_x in range(3):
            for shift_z in range(3):
                row = (x + shift_x) * PAD_Z + z + shift_z
                for side in range(2):
                    mx, my, mz, norm, weight = [
                        wide(source_ref[PLANES * side + c, pl.ds(row, 1), :]) for c in range(PLANES)
                    ]
                    for u in range(STEP):
                        for n in (0, 1) if side == 0 else (2,):
                            tx, ty, tz, own_norm = targets[u][n]
                            d2 = (own_norm + norm) + tx * mx + ty * my + tz * mz
                            value = weight * lax.rsqrt(d2)
                            if side == 0 and shift_x == 1 and shift_z == 1:
                                itself = lanes == slots + (8 * (STEP * step + u) + PPL * n)
                                value = jnp.where(itself, 0.0, value)
                            old = sums[u][n]
                            sums[u][n] = value if old is None else old + value
        for u in range(STEP):
            low, high, mixed = sums[u]
            start = pl.multiple_of(8 * (STEP * step + u), 8)
            sum_ref[leaf, pl.ds(start, 8), :] = low + jnp.where(lower_half, mixed, 0.0)
            sum_ref[leaf, pl.ds(PPL + start, 8), :] = high + jnp.where(lower_half, 0.0, mixed)

    def one_leaf_pair(leaf, carry):
        x = leaf // LZ
        z = leaf % LZ
        held = jnp.maximum(fill_ref[x * 2 * LZ + z], fill_ref[(x * 2 + 1) * LZ + z])

        def more(step, inner):
            add_tiles(leaf, step)
            return inner

        lax.fori_loop(0, (held + 8 * STEP - 1) // (8 * STEP), more, 0)
        return carry

    lax.fori_loop(0, LEAVES, one_leaf_pair, 0)
    ones = jnp.ones((2 * LANES, LANES), jnp.bfloat16)
    diagonal = lax.broadcasted_iota(jnp.int32, (LANES, LANES), 0) == lax.broadcasted_iota(
        jnp.int32, (LANES, LANES), 1
    )

    def finish(group, carry):
        rows = []
        for n in range(8):
            whole = sum_ref[8 * group + n]
            coarse = whole.astype(jnp.bfloat16)
            fine = (whole - coarse.astype(jnp.float32)).astype(jnp.bfloat16)
            added = jnp.dot(
                jnp.concatenate([coarse, fine], axis=1), ones, preferred_element_type=jnp.float32
            )
            rows.append(jnp.sum(jnp.where(diagonal, added, 0.0), axis=0, keepdims=True))
        out_ref[pl.ds(pl.multiple_of(8 * group, 8), 8), :] = jnp.concatenate(rows, axis=0)
        return carry

    lax.fori_loop(0, LEAVES // 8, finish, 0)


def near_sums(fill, sources, columns):
    return pl.pallas_call(
        near_kernel,
        out_shape=jax.ShapeDtypeStruct((LEAVES, LANES), jnp.float32),
        in_specs=[pl.BlockSpec(memory_space=pltpu.SMEM)]
        + [pl.BlockSpec(memory_space=pltpu.VMEM)] * 3,
        out_specs=pl.BlockSpec(memory_space=pltpu.VMEM),
        scratch_shapes=[
            pltpu.VMEM((LEAVES, LANES, LANES), jnp.float32),
            pltpu.VMEM((LZ, CXL * PPL, 3 * CYL * LANES), jnp.float32),
        ],
        compiler_params=pltpu.CompilerParams(vmem_limit_bytes=20 * 2**20),
        name="near_sums",
    )(fill, sources, columns, choices())


def extended(cells, sides, width):
    for axis, dim in sides:
        count = lax.axis_size(axis)
        even = lax.axis_index(axis) % 2 == 0
        head = lax.slice_in_dim(cells, 0, width, axis=dim)
        tail = lax.slice_in_dim(cells, cells.shape[dim] - width, cells.shape[dim], axis=dim)
        first = [(i, i ^ 1) for i in range(count)]
        second = [(i, i + 1 if i % 2 else i - 1) for i in range(1, count - 1)]
        inside = lax.ppermute(jnp.where(even, tail, head), axis, first)
        outside = lax.ppermute(jnp.where(even, head, tail), axis, second)
        cells = jnp.concatenate(
            [jnp.where(even, outside, inside), cells, jnp.where(even, inside, outside)], axis=dim
        )
    return cells


def live_charges(charges, counts):
    size_x, size_y = (counts.shape[0], counts.shape[1])
    filled = jnp.broadcast_to(counts[..., None], (size_x, size_y, LZ, PPL)).reshape(
        size_x, size_y, SLOTS
    )
    within = jnp.arange(SLOTS, dtype=jnp.int32) % PPL
    occupied = within[None, None, :] < filled
    return (jnp.where(occupied, charges, 0.0), occupied)


def placed(rows, start_x, start_y, start_z):
    size_x, size_y = rows.shape[1:3]
    along_x = (start_x + jnp.arange(size_x)).astype(jnp.float32)
    along_y = (start_y + jnp.arange(size_y)).astype(jnp.float32)
    along_z = (start_z + jnp.arange(SLOTS) // PPL).astype(jnp.float32)
    return jnp.stack(
        [
            rows[0] + along_x[:, None, None],
            rows[1] + along_y[None, :, None],
            rows[2] + along_z[None, None, :],
            rows[3],
        ]
    )


def leaf_pairs(cells):
    lead, size_x = cells.shape[:2]
    split = cells.reshape(lead, size_x, 2, LZ, PPL).transpose(0, 1, 3, 2, 4)
    return split.reshape(lead, size_x, LZ, LANES)


def per_device(positions, charges, counts, up_ops, m2l_ops, down_ops, box_lists):
    index_x = lax.axis_index("gx")
    index_y = lax.axis_index("gy")
    devices_x = lax.axis_size("gx")
    devices_y = lax.axis_size("gy")
    weights, occupied = live_charges(charges, counts)
    local_rows = jnp.concatenate([positions, weights[None]], axis=0)
    padded = extended(local_rows, (("gx", 1), ("gy", 2)), 1)

    own = placed(local_rows, 0, 0, 0)
    points = leaf_pairs(own).reshape(4, ROWS, LANES)
    held = leaf_pairs(occupied.astype(jnp.float32)[None]).reshape(ROWS, LANES)
    offsets = [devices_x * (devices_y - (devices_y >> h - 1)) for h in range(1, LEV + 1)]
    meta = jnp.concatenate([jnp.stack([index_x, index_y])] + [box_lists[o] for o in offsets])
    lattice = jnp.asarray(LATTICE, dtype=jnp.float32)
    sy = jnp.concatenate(
        [
            ((index_y >> h) * CYL * 2**h - index_y * CYL).astype(jnp.float32)
            + (0.5 * CYL * 2**h) * (1.0 + SURFACE_REACH * lattice)
            for h in range(1, LEV + 1)
        ]
    )
    sent = send_panels(meta, sy, points, up_ops, m2l_ops, down_ops, devices_x, devices_y)
    parts = lax.all_to_all(sent, ("gx", "gy"), split_axis=0, concat_axis=0, tiled=True)

    around = placed(padded, -1 - CXL // 2, -1 - CYL // 2, -(LZ // 2))
    norm = jnp.sum(square(around[:3]), axis=0, keepdims=True) + SOFTENING
    planes = jnp.concatenate([-2.0 * around[:3], norm, around[3:]])
    sides = [planes[:, :, 1:3], jnp.stack([planes[:, :, 0], planes[:, :, 3]], axis=2)]
    sources = jnp.concatenate([leaf_pairs(side) for side in sides])
    sources = jnp.pad(sources, ((0, 0), (0, 0), (1, 1), (0, 0)), constant_values=0.0)
    beyond = jnp.pad(jnp.zeros((LZ,), jnp.float32), (1, 1), constant_values=1.0)
    is_norm = (jnp.arange(2 * PLANES) % PLANES == 3).astype(jnp.float32)
    sources = sources + is_norm[:, None, None, None] * beyond[None, None, :, None]
    sources = sources.reshape(2 * PLANES, (CXL + 2) * PAD_Z, LANES)
    columns = placed(local_rows, -(CXL // 2), -(CYL // 2), -(LZ // 2))[:3]
    columns = columns.reshape(3, CXL, CYL, LZ, PPL).transpose(1, 4, 0, 2, 3)
    columns = columns.reshape(CXL * PPL, COLUMNS)
    columns = jnp.concatenate([columns] * 3 + [jnp.zeros((CXL * PPL, 2 * LANES - 3 * COLUMNS))], 1)
    fill = counts.reshape(-1)
    near = near_sums(fill, sources, columns)
    total = far_and_sum(sy, points, held, near, parts)
    total = total.reshape(CXL, LZ, CYL, PPL).transpose(0, 2, 1, 3)
    return total.reshape(CXL, CYL, SLOTS)


def solution(mesh):
    return jax.shard_map(
        per_device,
        mesh=mesh,
        in_specs=(
            P(None, "gx", "gy", None),
            P("gx", "gy", None),
            P("gx", "gy", None),
            P(),
            P(),
            P(),
            P(),
        ),
        out_specs=P("gx", "gy", None),
        check_vma=False,
    )
```

```python
import functools
import jax
import jax.numpy as jnp
import numpy as np
from jax import lax
from jax.experimental import pallas as pl
from jax.experimental.pallas import tpu as pltpu
from jax.sharding import PartitionSpec as P

CXL = 8
CYL = 2
LZ = 8
PPL = 64
P_ORD = 8
K = 8
LEV = 3
NE = 296
SLOTS = LZ * PPL
LANES = 128
ROWS = CXL * CYL * SLOTS // LANES
SOFTENING = 0.01
SURFACE_REACH = 1.05
PRECISE = lax.Precision.HIGHEST
LATTICE = np.linspace(-1.0, 1.0, P_ORD)
CHUNKS = ((0, 128), (128, 256), (256, NE))
INNER = range(1, P_ORD - 1)
ENDS = (0, P_ORD - 1)
A_TILES = [(a, b) for a in ENDS for b in range(P_ORD)]
B_TILES = [(a, b) for b in ENDS for a in INNER]
C_TILES = [(b, c) for c in ENDS for b in INNER]


def first_row(a, b):
    if a == 0:
        return 8 * b
    if a == P_ORD - 1:
        return 232 + 8 * b
    return 64 + 28 * (a - 1) + (0 if b == 0 else 20)


def strided_rows(b, c):
    return pl.ds(64 + 8 + 2 * (b - 1) + (1 if c else 0), P_ORD - 2, stride=28)


def lattice_y(h):
    index_y = lax.axis_index("gy")
    base = (((index_y >> h) << h) - index_y) * CYL
    span = CYL * 2**h
    return [
        base.astype(jnp.float32)
        + float(0.5 * span * (1.0 + SURFACE_REACH * LATTICE[b]) - 0.5 * CYL)
        for b in range(P_ORD)
    ]


def wide(row):
    return jnp.broadcast_to(row, (8, LANES))


def lattice_x(a):
    return float(SURFACE_REACH * 0.5 * CXL * LATTICE[a])


def lattice_z(c):
    return float(SURFACE_REACH * 0.5 * LZ * LATTICE[c])


def along_sublanes(half):
    steps = lax.broadcasted_iota(jnp.int32, (8, LANES), 0).astype(jnp.float32)
    return steps * (SURFACE_REACH * half * 2.0 / (P_ORD - 1)) - SURFACE_REACH * half


def square(value):
    return value * value


def a_squares(x8, z8, y_parts):
    along_z = square(along_sublanes(0.5 * LZ) - z8) + SOFTENING
    for a in ENDS:
        base = square(lattice_x(a) - x8) + along_z
        for b in range(P_ORD):
            yield base + y_parts[b]


def bc_squares(x8, z8, y_parts):
    along_z = square(along_sublanes(0.5 * LZ) - z8) + SOFTENING
    bases = [square(lattice_x(a) - x8) + along_z for a in INNER]
    for b in ENDS:
        for base in bases:
            yield base + y_parts[b]
    along_x = square(along_sublanes(0.5 * CXL) - x8) + SOFTENING
    for c in ENDS:
        base = along_x + square(lattice_z(c) - z8)
        for b in INNER:
            yield base + y_parts[b]


def row_of(p_ref, r):
    return [wide(p_ref[c, pl.ds(r, 1), :]) for c in range(p_ref.shape[0])]


def send_kernel(
    span_x, span_y, lists_ref, counts_ref, positions_ref, charges_ref, up_hbm, m2l_hbm, down_hbm,
    out_ref, p_ref, up_ref, m2l_ref, down_ref, check_ref, row_ref, column_ref, panel_ref, sems,
):
    copies = [pltpu.make_async_copy(up_hbm, up_ref, sems.at[0])]
    copies += [
        pltpu.make_async_copy(m2l_hbm.at[h], m2l_ref.at[h], sems.at[1 + h]) for h in range(LEV)
    ]
    copies.append(pltpu.make_async_copy(down_hbm, down_ref, sems.at[1 + LEV]))
    for copy in copies:
        copy.start()
    row_ref[...] = jnp.zeros((8, 384), jnp.float32)
    lane = lax.broadcasted_iota(jnp.int32, (CYL, LANES), 1)
    upper = lane // PPL
    slot = lane % PPL
    along_y = lax.broadcasted_iota(jnp.int32, (CYL, LANES), 0)
    for x in range(CXL):
        for q in range(SLOTS // LANES):
            here = slice(LANES * q, LANES * (q + 1))
            rows = slice(8 * x + CYL * q, 8 * x + CYL * (q + 1))
            place_z = (upper + (2 * q - LZ // 2)).astype(jnp.float32)
            p_ref[0, rows, :] = positions_ref[0, x, :, here] + float(x - CXL // 2)
            p_ref[1, rows, :] = positions_ref[1, x, :, here] + (along_y - 1).astype(jnp.float32)
            p_ref[2, rows, :] = positions_ref[2, x, :, here] + place_z
            held = [
                jnp.where(
                    upper == 0,
                    counts_ref[(x * CYL + y) * LZ + 2 * q],
                    counts_ref[(x * CYL + y) * LZ + 2 * q + 1],
                )
                for y in range(CYL)
            ]
            held = jnp.where(along_y == 0, held[0], held[1])
            p_ref[3, rows, :] = jnp.where(slot < held, charges_ref[x, :, here], 0.0)

    for h in range(LEV):
        ys = lattice_y(h + 1)
        for squares, tiles in ((a_squares, A_TILES), (bc_squares, B_TILES + C_TILES)):

            def gather(r, sums):
                x8, y8, z8, w8 = row_of(p_ref, r)
                y_parts = [square(ys[b] - y8) for b in range(P_ORD)]
                return [
                    total + w8 * lax.rsqrt(d2)
                    for total, d2 in zip(sums, squares(x8, z8, y_parts))
                ]

            sums = lax.fori_loop(
                0, ROWS, gather, [jnp.zeros((8, LANES), jnp.float32) for _ in tiles], unroll=2
            )
            for n, (total, tile) in enumerate(zip(sums, tiles)):
                filled = jnp.broadcast_to(jnp.sum(total, axis=1, keepdims=True), (8, LANES))
                if squares is bc_squares and n >= len(B_TILES):
                    check_ref[h, strided_rows(*tile), :] = filled[1:7]
                else:
                    check_ref[h, pl.ds(first_row(*tile), 8), :] = filled

    copies[0].wait()
    for h in range(LEV):
        for low, high in CHUNKS:
            total = jnp.zeros((8, high - low), jnp.float32)
            for i in range(0, NE, 8):
                total += check_ref[h, i : i + 8, : high - low] * up_ref[h, i : i + 8, low:high]
            row_ref[h : h + 1, low:high] = jnp.sum(total, axis=0, keepdims=True)
    flipped = jnp.transpose(row_ref[...])
    for h in range(LEV):
        column_ref[h] = jnp.broadcast_to(flipped[:NE, h : h + 1], (NE, LANES))

    for h in range(LEV):
        copies[1 + h].wait()

        def translate(k, carry):
            for low, high in CHUNKS:
                total = jnp.zeros((8, high - low), jnp.float32)
                for i in range(0, NE, 8):
                    total += (
                        column_ref[h, i : i + 8, : high - low]
                        * m2l_ref[h, k, i : i + 8, low:high]
                    )
                panel_ref[h, k, :, low:high] = total
            return carry

        lax.fori_loop(0, K, translate, 0)

    copies[1 + LEV].wait()
    panels = [jnp.sum(panel_ref[h], axis=1) for h in range(LEV)]
    top = panels[2]
    middle = jnp.concatenate(
        [panels[1]]
        + [
            jnp.dot(top, down_ref[1, side], precision=PRECISE, preferred_element_type=jnp.float32)
            for side in range(2)
        ],
        axis=0,
    )
    lower = [
        jnp.dot(middle, down_ref[0, side], precision=PRECISE, preferred_element_type=jnp.float32)
        for side in range(2)
    ]
    out_ref[...] = jnp.zeros(out_ref.shape, jnp.float32)
    index_x = lax.axis_index("gx")
    index_y = lax.axis_index("gy")
    for h in range(1, LEV + 1):
        offset = span_x * (span_y - (span_y >> h - 1))
        across = span_y >> h
        bits = across.bit_length() - 1
        own_box = (index_x << bits) + (index_y >> h)
        for k in range(K):
            box = (own_box - lists_ref[offset, k]) & (span_x * across - 1)
            first = (box >> bits) * span_y + ((box & (across - 1)) << h)
            for j in range(2**h):
                if h == 1:
                    value = panels[0][k : k + 1]
                else:
                    start = 8 * (h - 2 + j // 4) + k
                    value = lower[j // 2 % 2][start : start + 1]
                out_ref[first + j] += value


def send_panels(lists, counts, positions, charges, up_ops, m2l_ops, down_ops, span_x, span_y):
    return pl.pallas_call(
        functools.partial(send_kernel, span_x, span_y),
        out_shape=jax.ShapeDtypeStruct((span_x * span_y, 1, NE), jnp.float32),
        in_specs=[
            pl.BlockSpec(memory_space=pltpu.SMEM),
            pl.BlockSpec(memory_space=pltpu.SMEM),
            pl.BlockSpec(memory_space=pltpu.VMEM),
            pl.BlockSpec(memory_space=pltpu.VMEM),
            pl.BlockSpec(memory_space=pltpu.HBM),
            pl.BlockSpec(memory_space=pltpu.HBM),
            pl.BlockSpec(memory_space=pltpu.HBM),
        ],
        out_specs=pl.BlockSpec(memory_space=pltpu.VMEM),
        scratch_shapes=[
            pltpu.VMEM((4, ROWS, LANES), jnp.float32),
            pltpu.VMEM((LEV, NE, NE), jnp.float32),
            pltpu.VMEM((LEV, K, NE, NE), jnp.float32),
            pltpu.VMEM((LEV - 1, 2, NE, NE), jnp.float32),
            pltpu.VMEM((LEV, NE, LANES), jnp.float32),
            pltpu.VMEM((8, 384), jnp.float32),
            pltpu.VMEM((LEV, NE, LANES), jnp.float32),
            pltpu.VMEM((LEV, K, 8, NE), jnp.float32),
            pltpu.SemaphoreType.DMA((LEV + 2,)),
        ],
        compiler_params=pltpu.CompilerParams(vmem_limit_bytes=46 * 2**20),
        name="send_panels",
    )(lists, counts, positions, charges, up_ops, m2l_ops, down_ops)


def far_kernel(points_ref, near_ref, parts_ref, out_ref, row_ref, column_ref, tile_ref):
    row_ref[...] = jnp.zeros((8, 384), jnp.float32)
    row_ref[0:1, :NE] = jnp.sum(parts_ref[...], axis=0)
    flipped = jnp.transpose(row_ref[...])
    column_ref[...] = jnp.broadcast_to(flipped[:NE, 0:1], (NE, LANES))
    for n, tile in enumerate(A_TILES + B_TILES):
        tile_ref[n] = column_ref[pl.ds(first_row(*tile), 8), :]
    for n, tile in enumerate(C_TILES):
        n += len(A_TILES + B_TILES)
        tile_ref[n] = jnp.zeros((8, LANES), jnp.float32)
        tile_ref[n, 1:7, :] = column_ref[strided_rows(*tile), :]
    ys = lattice_y(1)
    lower_half = lax.broadcasted_iota(jnp.int32, (1, LANES), 1) < PPL

    def potential(r):
        x8, y8, z8, held = row_of(points_ref, r)
        y_parts = [square(ys[b] - y8) for b in range(P_ORD)]
        totals = [jnp.zeros((8, LANES), jnp.float32) for _ in range(4)]
        n = 0
        for squares in (a_squares, bc_squares):
            for d2 in squares(x8, z8, y_parts):
                totals[n % 4] += tile_ref[n] * lax.rsqrt(d2)
                n += 1
        far = jnp.sum(totals[0] + totals[1] + (totals[2] + totals[3]), axis=0, keepdims=True)
        return jnp.where(held[0:1] > 0, near_ref[pl.ds(r, 1), :] + far, 0.0)

    def one_x(x, carry):
        for q in range(LZ // 2):
            first = potential(x * LZ + 2 * q)
            second = potential(x * LZ + 2 * q + 1)
            here = slice(LANES * q, LANES * (q + 1))
            turned = pltpu.roll(second, PPL, 1)
            out_ref[x, 0:1, here] = jnp.where(lower_half, first, turned)
            turned = pltpu.roll(first, PPL, 1)
            out_ref[x, 1:2, here] = jnp.where(lower_half, turned, second)
        return carry

    lax.fori_loop(0, CXL, one_x, 0)


def far_and_sum(points, near, parts):
    return pl.pallas_call(
        far_kernel,
        out_shape=jax.ShapeDtypeStruct((CXL, CYL, SLOTS), jnp.float32),
        in_specs=[pl.BlockSpec(memory_space=pltpu.VMEM)] * 3,
        out_specs=pl.BlockSpec(memory_space=pltpu.VMEM),
        scratch_shapes=[
            pltpu.VMEM((8, 384), jnp.float32),
            pltpu.VMEM((NE, LANES), jnp.float32),
            pltpu.VMEM((40, 8, LANES), jnp.float32),
        ],
        compiler_params=pltpu.CompilerParams(vmem_limit_bytes=16 * 2**20),
        name="far_and_sum",
    )(points, near, parts)


PAD_Z = LZ + 2
PLANES = 5
STEP = 2
TILES = PPL // 8
LEAVES = CXL * LZ
PARTS = 3
CHOICE = 3 * LZ


def near_kernel(
    fill_ref, table_ref, out_ref, points_ref, source_ref, sum_ref, turn_ref, place_ref
):
    lanes = lax.broadcasted_iota(jnp.int32, (8, LANES), 1)
    slots = lax.broadcasted_iota(jnp.int32, (8, LANES), 0)
    lower_half = lanes < PPL
    wide_x = CXL + 2
    lane = lax.broadcasted_iota(jnp.int32, (wide_x, LANES), 1)
    lower = lane < PPL
    along_x = lax.broadcasted_iota(jnp.int32, (wide_x, LANES), 0)
    along_x = (along_x - (1 + CXL // 2)).astype(jnp.float32)
    for plane in range(2 * PLANES):
        value = 1.0 if plane % PLANES == 3 else 0.0
        source_ref[plane] = jnp.full(source_ref.shape[1:], value, jnp.float32)
    for side, (first, second) in enumerate(((1, 2), (0, 3))):
        along_y = jnp.where(lower, float(first - 2), float(second - 2))
        for z in range(LZ):
            here = slice(z // 2 * LANES, (z // 2 + 1) * LANES)

            def both(c):
                one = table_ref[first, c, :, here]
                two = table_ref[second, c, :, here]
                if z % 2:
                    one = pltpu.roll(one, PPL, 1)
                else:
                    two = pltpu.roll(two, PPL, 1)
                return jnp.where(lower, one, two)

            held = jnp.where(
                lower,
                jnp.broadcast_to(table_ref[first, 4, :, z : z + 1], (wide_x, LANES)),
                jnp.broadcast_to(table_ref[second, 4, :, z : z + 1], (wide_x, LANES)),
            )
            held = (lane % PPL).astype(jnp.float32) < held
            coords = [both(0) + along_x, both(1) + along_y, both(2) + float(z - LZ // 2)]
            norm = square(coords[0]) + square(coords[1]) + square(coords[2]) + SOFTENING
            planes = [-2.0 * coord for coord in coords]
            planes += [norm, jnp.where(held, both(3), 0.0)]
            for n, plane in enumerate(planes):
                source_ref[PLANES * side + n, pl.ds(z + 1, wide_x, stride=PAD_Z), :] = plane
            if side == 0:
                for n, plane in enumerate(coords + [held.astype(jnp.float32)]):
                    points_ref[n, pl.ds(z, CXL, stride=LZ), :] = plane[1 : CXL + 1]

    turn_ref[...] = jnp.zeros(turn_ref.shape, jnp.float32)
    tables = [[], []]
    for x in range(CXL):
        rest = jnp.concatenate([points_ref[c, x * LZ : (x + 1) * LZ, :] for c in range(3)], axis=0)
        for part in range(PARTS):
            rounded = rest.astype(jnp.bfloat16).astype(jnp.float32)
            turn_ref[CHOICE * part : CHOICE * (part + 1), :] = rounded
            rest = rest - rounded
        turned = jnp.transpose(turn_ref[...]).astype(jnp.bfloat16)
        for y in range(CYL):
            tables[y].append(turned[PPL * y : PPL * (y + 1)])
    tables = [jnp.concatenate(table, axis=0) for table in tables]
    row = lax.broadcasted_iota(jnp.int32, (LANES, LANES), 0)
    row = jnp.where(row < PARTS * CHOICE, row % CHOICE, -1)
    for z in range(LZ):
        chosen = jnp.concatenate(
            [(row == c * LZ + z).astype(jnp.float32) for c in range(3)], axis=1
        ).astype(jnp.bfloat16)
        for y in range(CYL):
            place_ref[y, z] = jnp.dot(tables[y], chosen, preferred_element_type=jnp.float32)

    def add_tiles(leaf, step):
        x = leaf // LZ
        z = leaf % LZ
        targets = []
        for u in range(STEP):
            start = pl.multiple_of(x * PPL + 8 * (STEP * step + u), 8)
            low, high = [
                [
                    place_ref[y, z, pl.ds(start, 8), LANES * c : LANES * (c + 1)]
                    for c in range(3)
                ]
                for y in range(CYL)
            ]
            for place in (low, high):
                place.append(square(place[0]) + square(place[1]) + square(place[2]))
            mixed = [jnp.where(lower_half, l, h) for l, h in zip(low, high)]
            targets.append((low, high, mixed))
        sums = [[None] * 3 for _ in range(STEP)]
        for shift_x in range(3):
            for shift_z in range(3):
                row = (x + shift_x) * PAD_Z + z + shift_z
                for side in range(2):
                    mx, my, mz, norm, weight = [
                        wide(source_ref[PLANES * side + c, pl.ds(row, 1), :]) for c in range(PLANES)
                    ]
                    for u in range(STEP):
                        for n in (0, 1) if side == 0 else (2,):
                            tx, ty, tz, own_norm = targets[u][n]
                            d2 = (own_norm + norm) + tx * mx + ty * my + tz * mz
                            value = weight * lax.rsqrt(d2)
                            if side == 0 and shift_x == 1 and shift_z == 1:
                                itself = lanes == slots + (8 * (STEP * step + u) + PPL * n)
                                value = jnp.where(itself, 0.0, value)
                            old = sums[u][n]
                            sums[u][n] = value if old is None else old + value
        for u in range(STEP):
            low, high, mixed = sums[u]
            start = pl.multiple_of(8 * (STEP * step + u), 8)
            sum_ref[leaf, pl.ds(start, 8), :] = low + jnp.where(lower_half, mixed, 0.0)
            sum_ref[leaf, pl.ds(PPL + start, 8), :] = high + jnp.where(lower_half, 0.0, mixed)

    def one_leaf_pair(leaf, carry):
        x = leaf // LZ
        z = leaf % LZ
        held = jnp.maximum(fill_ref[x * 2 * LZ + z], fill_ref[(x * 2 + 1) * LZ + z])

        def more(step, inner):
            add_tiles(leaf, step)
            return inner

        lax.fori_loop(0, (held + 8 * STEP - 1) // (8 * STEP), more, 0)
        return carry

    lax.fori_loop(0, LEAVES, one_leaf_pair, 0)
    ones = jnp.ones((2 * LANES, LANES), jnp.bfloat16)
    diagonal = lax.broadcasted_iota(jnp.int32, (LANES, LANES), 0) == lax.broadcasted_iota(
        jnp.int32, (LANES, LANES), 1
    )

    def finish(group, carry):
        rows = []
        for n in range(8):
            whole = sum_ref[8 * group + n]
            coarse = whole.astype(jnp.bfloat16)
            fine = (whole - coarse.astype(jnp.float32)).astype(jnp.bfloat16)
            added = jnp.dot(
                jnp.concatenate([coarse, fine], axis=1), ones, preferred_element_type=jnp.float32
            )
            rows.append(jnp.sum(jnp.where(diagonal, added, 0.0), axis=0, keepdims=True))
        out_ref[pl.ds(pl.multiple_of(8 * group, 8), 8), :] = jnp.concatenate(rows, axis=0)
        return carry

    lax.fori_loop(0, LEAVES // 8, finish, 0)


def near_sums(fill, table):
    return pl.pallas_call(
        near_kernel,
        out_shape=(
            jax.ShapeDtypeStruct((LEAVES, LANES), jnp.float32),
            jax.ShapeDtypeStruct((4, LEAVES, LANES), jnp.float32),
        ),
        in_specs=[
            pl.BlockSpec(memory_space=pltpu.SMEM),
            pl.BlockSpec(memory_space=pltpu.VMEM),
        ],
        out_specs=(
            pl.BlockSpec(memory_space=pltpu.VMEM),
            pl.BlockSpec(memory_space=pltpu.VMEM),
        ),
        scratch_shapes=[
            pltpu.VMEM((2 * PLANES, (CXL + 2) * PAD_Z, LANES), jnp.float32),
            pltpu.VMEM((LEAVES, LANES, LANES), jnp.float32),
            pltpu.VMEM((LANES, LANES), jnp.float32),
            pltpu.VMEM((CYL, LZ, CXL * PPL, 3 * LANES), jnp.float32),
        ],
        compiler_params=pltpu.CompilerParams(vmem_limit_bytes=28 * 2**20),
        name="near_sums",
    )(fill, table)


def extended(cells, sides, width):
    for axis, dim in sides:
        count = lax.axis_size(axis)
        even = lax.axis_index(axis) % 2 == 0
        head = lax.slice_in_dim(cells, 0, width, axis=dim)
        tail = lax.slice_in_dim(cells, cells.shape[dim] - width, cells.shape[dim], axis=dim)
        first = [(i, i ^ 1) for i in range(count)]
        second = [(i, i + 1 if i % 2 else i - 1) for i in range(1, count - 1)]
        inside = lax.ppermute(jnp.where(even, tail, head), axis, first)
        outside = lax.ppermute(jnp.where(even, head, tail), axis, second)
        cells = jnp.concatenate(
            [jnp.where(even, outside, inside), cells, jnp.where(even, inside, outside)], axis=dim
        )
    return cells


def per_device(positions, charges, counts, up_ops, m2l_ops, down_ops, box_lists):
    devices_x = lax.axis_size("gx")
    devices_y = lax.axis_size("gy")
    filled = jnp.pad(counts.astype(jnp.float32), ((0, 0), (0, 0), (0, SLOTS - LZ)))
    rows = jnp.concatenate([positions, charges[None], filled[None]], axis=0)
    padded = extended(rows, (("gx", 1), ("gy", 2)), 1)
    fill = counts.reshape(-1)
    sent = send_panels(
        box_lists, fill, positions, charges, up_ops, m2l_ops, down_ops, devices_x, devices_y
    )
    parts = lax.all_to_all(sent, ("gx", "gy"), split_axis=0, concat_axis=0, tiled=True)
    near, points = near_sums(fill, padded.transpose(2, 0, 1, 3))
    return far_and_sum(points, near, parts)


def solution(mesh):
    return jax.shard_map(
        per_device,
        mesh=mesh,
        in_specs=(
            P(None, "gx", "gy", None),
            P("gx", "gy", None),
            P("gx", "gy", None),
            P(),
            P(),
            P(),
            P(),
        ),
        out_specs=P("gx", "gy", None),
        check_vma=False,
    )
```

```python
import functools
import jax
import jax.numpy as jnp
import numpy as np
from jax import lax
from jax.experimental import pallas as pl
from jax.experimental.pallas import tpu as pltpu
from jax.sharding import PartitionSpec as P

CXL = 8
CYL = 2
LZ = 8
PPL = 64
P_ORD = 8
K = 8
LEV = 3
NE = 296
SLOTS = LZ * PPL
LANES = 128
GRANT = 58
ROWS = CXL * CYL * SLOTS // LANES
SOFTENING = 0.01
SURFACE_REACH = 1.05
PRECISE = lax.Precision.HIGHEST
LATTICE = np.linspace(-1.0, 1.0, P_ORD)
CHUNKS = ((0, 128), (128, 256), (256, NE))
INNER = range(1, P_ORD - 1)
ENDS = (0, P_ORD - 1)
A_TILES = [(a, b) for a in ENDS for b in range(P_ORD)]
B_TILES = [(a, b) for b in ENDS for a in INNER]
C_TILES = [(b, c) for c in ENDS for b in INNER]


def first_row(a, b):
    if a == 0:
        return 8 * b
    if a == P_ORD - 1:
        return 232 + 8 * b
    return 64 + 28 * (a - 1) + (0 if b == 0 else 20)


def strided_rows(b, c):
    return pl.ds(64 + 8 + 2 * (b - 1) + (1 if c else 0), P_ORD - 2, stride=28)


def lattice_y(h):
    index_y = lax.axis_index("gy")
    base = (((index_y >> h) << h) - index_y) * CYL
    span = CYL * 2**h
    return [
        base.astype(jnp.float32)
        + float(0.5 * span * (1.0 + SURFACE_REACH * LATTICE[b]) - 0.5 * CYL)
        for b in range(P_ORD)
    ]


def wide(row):
    return jnp.broadcast_to(row, (8, LANES))


def lattice_x(a):
    return float(SURFACE_REACH * 0.5 * CXL * LATTICE[a])


def lattice_z(c):
    return float(SURFACE_REACH * 0.5 * LZ * LATTICE[c])


def along_sublanes(half):
    steps = lax.broadcasted_iota(jnp.int32, (8, LANES), 0).astype(jnp.float32)
    return steps * (SURFACE_REACH * half * 2.0 / (P_ORD - 1)) - SURFACE_REACH * half


def square(value):
    return value * value


def a_squares(x8, z8, y_parts):
    along_z = square(along_sublanes(0.5 * LZ) - z8) + SOFTENING
    for a in ENDS:
        base = square(lattice_x(a) - x8) + along_z
        for b in range(P_ORD):
            yield base + y_parts[b]


def bc_squares(x8, z8, y_parts):
    along_z = square(along_sublanes(0.5 * LZ) - z8) + SOFTENING
    bases = [square(lattice_x(a) - x8) + along_z for a in INNER]
    for b in ENDS:
        for base in bases:
            yield base + y_parts[b]
    along_x = square(along_sublanes(0.5 * CXL) - x8) + SOFTENING
    for c in ENDS:
        base = along_x + square(lattice_z(c) - z8)
        for b in INNER:
            yield base + y_parts[b]


def row_of(p_ref, r):
    return [wide(p_ref[c, pl.ds(r, 1), :]) for c in range(p_ref.shape[0])]


def fill_points(own_ref, p_ref):
    lane = lax.broadcasted_iota(jnp.int32, (CXL, LANES), 1)
    upper = lane // PPL
    slot = (lane % PPL).astype(jnp.float32)
    along_x = lax.broadcasted_iota(jnp.int32, (CXL, LANES), 0) - CXL // 2
    for y in range(CYL):
        for q in range(SLOTS // LANES):
            here = slice(LANES * q, LANES * (q + 1))
            rows = slice(CXL * (4 * y + q), CXL * (4 * y + q + 1))
            place_z = (upper + (2 * q - LZ // 2)).astype(jnp.float32)
            p_ref[0, rows, :] = own_ref[y, 0, :, here] + along_x.astype(jnp.float32)
            p_ref[1, rows, :] = own_ref[y, 1, :, here] + float(y - CYL // 2)
            p_ref[2, rows, :] = own_ref[y, 2, :, here] + place_z
            held = [
                jnp.broadcast_to(own_ref[y, 4, :, z : z + 1], (CXL, LANES))
                for z in (2 * q, 2 * q + 1)
            ]
            held = jnp.where(upper == 0, held[0], held[1])
            p_ref[3, rows, :] = jnp.where(slot < held, own_ref[y, 3, :, here], 0.0)


def add_checks(levels, p_ref, check_ref):
    for n, h in enumerate(levels):
        ys = lattice_y(h)
        for squares, tiles in ((a_squares, A_TILES), (bc_squares, B_TILES + C_TILES)):

            def gather(r, sums):
                x8, y8, z8, w8 = row_of(p_ref, r)
                y_parts = [square(ys[b] - y8) for b in range(P_ORD)]
                return [
                    total + w8 * lax.rsqrt(d2)
                    for total, d2 in zip(sums, squares(x8, z8, y_parts))
                ]

            sums = lax.fori_loop(
                0, ROWS, gather, [jnp.zeros((8, LANES), jnp.float32) for _ in tiles], unroll=2
            )
            for i, (total, tile) in enumerate(zip(sums, tiles)):
                filled = jnp.broadcast_to(jnp.sum(total, axis=1, keepdims=True), (8, LANES))
                if squares is bc_squares and i >= len(B_TILES):
                    check_ref[n, strided_rows(*tile), :] = filled[1:7]
                else:
                    check_ref[n, pl.ds(first_row(*tile), 8), :] = filled


def check_kernel(h, own_ref, check_ref, p_ref):
    fill_points(own_ref, p_ref)
    add_checks([h], p_ref, check_ref)


def one_check(h, own):
    return pl.pallas_call(
        functools.partial(check_kernel, h),
        out_shape=jax.ShapeDtypeStruct((1, NE, LANES), jnp.float32),
        in_specs=[pl.BlockSpec(memory_space=pltpu.VMEM)],
        out_specs=pl.BlockSpec(memory_space=pltpu.VMEM),
        scratch_shapes=[pltpu.VMEM((4, ROWS, LANES), jnp.float32)],
        compiler_params=pltpu.CompilerParams(vmem_limit_bytes=4 * 2**20),
        name="one_check",
    )(own)


def send_kernel(
    span_x, span_y, lists_ref, first_ref, second_ref, own_ref, up_hbm, m2l_hbm, down_hbm,
    out_ref, p_ref, up_ref, m2l_ref, down_ref, check_ref, row_ref, column_ref, panel_ref, sems,
):
    copies = [pltpu.make_async_copy(up_hbm, up_ref, sems.at[0])]
    copies += [
        pltpu.make_async_copy(m2l_hbm.at[h], m2l_ref.at[h], sems.at[1 + h]) for h in range(LEV)
    ]
    copies.append(pltpu.make_async_copy(down_hbm, down_ref, sems.at[1 + LEV]))
    for copy in copies:
        copy.start()
    row_ref[...] = jnp.zeros((8, 384), jnp.float32)
    fill_points(own_ref, p_ref)
    add_checks([LEV], p_ref, check_ref)
    copies[0].wait()
    for h in range(LEV):
        for low, high in CHUNKS:
            total = jnp.zeros((8, high - low), jnp.float32)
            for i in range(0, NE, 8):
                check = (first_ref, second_ref, check_ref)[h][0, i : i + 8, : high - low]
                total += check * up_ref[h, i : i + 8, low:high]
            row_ref[h : h + 1, low:high] = jnp.sum(total, axis=0, keepdims=True)
    flipped = jnp.transpose(row_ref[...])
    for h in range(LEV):
        column_ref[h] = jnp.broadcast_to(flipped[:NE, h : h + 1], (NE, LANES))

    for h in range(LEV):
        copies[1 + h].wait()

        def translate(k, carry):
            for low, high in CHUNKS:
                total = jnp.zeros((8, high - low), jnp.float32)
                for i in range(0, NE, 8):
                    total += (
                        column_ref[h, i : i + 8, : high - low]
                        * m2l_ref[h, k, i : i + 8, low:high]
                    )
                panel_ref[h, k, :, low:high] = total
            return carry

        lax.fori_loop(0, K, translate, 0)

    copies[1 + LEV].wait()
    panels = [jnp.sum(panel_ref[h], axis=1) for h in range(LEV)]
    top = panels[2]
    middle = jnp.concatenate(
        [panels[1]]
        + [
            jnp.dot(top, down_ref[1, side], precision=PRECISE, preferred_element_type=jnp.float32)
            for side in range(2)
        ],
        axis=0,
    )
    lower = [
        jnp.dot(middle, down_ref[0, side], precision=PRECISE, preferred_element_type=jnp.float32)
        for side in range(2)
    ]
    out_ref[...] = jnp.zeros(out_ref.shape, jnp.float32)
    index_x = lax.axis_index("gx")
    index_y = lax.axis_index("gy")
    for h in range(1, LEV + 1):
        offset = span_x * (span_y - (span_y >> h - 1))
        across = span_y >> h
        bits = across.bit_length() - 1
        own_box = (index_x << bits) + (index_y >> h)
        for k in range(K):
            box = (own_box - lists_ref[k, offset]) & (span_x * across - 1)
            first = (box >> bits) * span_y + ((box & (across - 1)) << h)
            for j in range(2**h):
                if h == 1:
                    value = panels[0][k : k + 1]
                else:
                    start = 8 * (h - 2 + j // 4) + k
                    value = lower[j // 2 % 2][start : start + 1]
                out_ref[first + j] += value


def send_panels(lists, first, second, own, up_ops, m2l_ops, down_ops, span_x, span_y):
    return pl.pallas_call(
        functools.partial(send_kernel, span_x, span_y),
        out_shape=jax.ShapeDtypeStruct((span_x * span_y, 1, NE), jnp.float32),
        in_specs=[
            pl.BlockSpec(memory_space=pltpu.SMEM),
            pl.BlockSpec(memory_space=pltpu.VMEM),
            pl.BlockSpec(memory_space=pltpu.VMEM),
            pl.BlockSpec(memory_space=pltpu.VMEM),
            pl.BlockSpec(memory_space=pltpu.HBM),
            pl.BlockSpec(memory_space=pltpu.HBM),
            pl.BlockSpec(memory_space=pltpu.HBM),
        ],
        out_specs=pl.BlockSpec(memory_space=pltpu.VMEM),
        scratch_shapes=[
            pltpu.VMEM((4, ROWS, LANES), jnp.float32),
            pltpu.VMEM((LEV, NE, NE), jnp.float32),
            pltpu.VMEM((LEV, K, NE, NE), jnp.float32),
            pltpu.VMEM((LEV - 1, 2, NE, NE), jnp.float32),
            pltpu.VMEM((1, NE, LANES), jnp.float32),
            pltpu.VMEM((8, 384), jnp.float32),
            pltpu.VMEM((LEV, NE, LANES), jnp.float32),
            pltpu.VMEM((LEV, K, 8, NE), jnp.float32),
            pltpu.SemaphoreType.DMA((LEV + 2,)),
        ],
        compiler_params=pltpu.CompilerParams(vmem_limit_bytes=GRANT * 2**20),
        name="send_panels",
    )(lists, first, second, own, up_ops, m2l_ops, down_ops)


def far_kernel(points_ref, near_ref, parts_ref, out_ref, row_ref, column_ref, tile_ref):
    row_ref[...] = jnp.zeros((8, 384), jnp.float32)
    row_ref[0:1, :NE] = jnp.sum(parts_ref[...], axis=0)
    flipped = jnp.transpose(row_ref[...])
    column_ref[...] = jnp.broadcast_to(flipped[:NE, 0:1], (NE, LANES))
    for n, tile in enumerate(A_TILES + B_TILES):
        tile_ref[n] = column_ref[pl.ds(first_row(*tile), 8), :]
    for n, tile in enumerate(C_TILES):
        n += len(A_TILES + B_TILES)
        tile_ref[n] = jnp.zeros((8, LANES), jnp.float32)
        tile_ref[n, 1:7, :] = column_ref[strided_rows(*tile), :]
    ys = lattice_y(1)
    lower_half = lax.broadcasted_iota(jnp.int32, (1, LANES), 1) < PPL

    def potential(r):
        x8, y8, z8, held = row_of(points_ref, r)
        y_parts = [square(ys[b] - y8) for b in range(P_ORD)]
        totals = [jnp.zeros((8, LANES), jnp.float32) for _ in range(4)]
        n = 0
        for squares in (a_squares, bc_squares):
            for d2 in squares(x8, z8, y_parts):
                totals[n % 4] += tile_ref[n] * lax.rsqrt(d2)
                n += 1
        far = jnp.sum(totals[0] + totals[1] + (totals[2] + totals[3]), axis=0, keepdims=True)
        return jnp.where(held[0:1] > 0, near_ref[pl.ds(r, 1), :] + far, 0.0)

    def one_x(x, carry):
        for q in range(LZ // 2):
            first = potential(x * LZ + 2 * q)
            second = potential(x * LZ + 2 * q + 1)
            here = slice(LANES * q, LANES * (q + 1))
            turned = pltpu.roll(second, PPL, 1)
            out_ref[x, 0:1, here] = jnp.where(lower_half, first, turned)
            turned = pltpu.roll(first, PPL, 1)
            out_ref[x, 1:2, here] = jnp.where(lower_half, turned, second)
        return carry

    lax.fori_loop(0, CXL, one_x, 0)


def far_and_sum(points, near, parts):
    return pl.pallas_call(
        far_kernel,
        out_shape=jax.ShapeDtypeStruct((CXL, CYL, SLOTS), jnp.float32),
        in_specs=[pl.BlockSpec(memory_space=pltpu.VMEM)] * 3,
        out_specs=pl.BlockSpec(memory_space=pltpu.VMEM),
        scratch_shapes=[
            pltpu.VMEM((8, 384), jnp.float32),
            pltpu.VMEM((NE, LANES), jnp.float32),
            pltpu.VMEM((40, 8, LANES), jnp.float32),
        ],
        compiler_params=pltpu.CompilerParams(vmem_limit_bytes=16 * 2**20),
        name="far_and_sum",
    )(points, near, parts)


PAD_Z = LZ + 2
PLANES = 5
STEP = 2
TILES = PPL // 8
LEAVES = CXL * LZ
PARTS = 3
CHOICE = 3 * LZ


def near_kernel(
    fill_ref, table_ref, out_ref, points_ref, source_ref, sum_ref, turn_ref, place_ref
):
    lanes = lax.broadcasted_iota(jnp.int32, (8, LANES), 1)
    slots = lax.broadcasted_iota(jnp.int32, (8, LANES), 0)
    lower_half = lanes < PPL
    wide_x = CXL + 2
    lane = lax.broadcasted_iota(jnp.int32, (wide_x, LANES), 1)
    lower = lane < PPL
    along_x = lax.broadcasted_iota(jnp.int32, (wide_x, LANES), 0)
    along_x = (along_x - (1 + CXL // 2)).astype(jnp.float32)
    for plane in range(2 * PLANES):
        value = 1.0 if plane % PLANES == 3 else 0.0
        source_ref[plane] = jnp.full(source_ref.shape[1:], value, jnp.float32)
    for side, (first, second) in enumerate(((1, 2), (0, 3))):
        along_y = jnp.where(lower, float(first - 2), float(second - 2))
        for z in range(LZ):
            here = slice(z // 2 * LANES, (z // 2 + 1) * LANES)

            def both(c):
                one = table_ref[first, c, :, here]
                two = table_ref[second, c, :, here]
                if z % 2:
                    one = pltpu.roll(one, PPL, 1)
                else:
                    two = pltpu.roll(two, PPL, 1)
                return jnp.where(lower, one, two)

            held = jnp.where(
                lower,
                jnp.broadcast_to(table_ref[first, 4, :, z : z + 1], (wide_x, LANES)),
                jnp.broadcast_to(table_ref[second, 4, :, z : z + 1], (wide_x, LANES)),
            )
            held = (lane % PPL).astype(jnp.float32) < held
            coords = [both(0) + along_x, both(1) + along_y, both(2) + float(z - LZ // 2)]
            norm = square(coords[0]) + square(coords[1]) + square(coords[2]) + SOFTENING
            planes = [-2.0 * coord for coord in coords]
            planes += [norm, jnp.where(held, both(3), 0.0)]
            for n, plane in enumerate(planes):
                source_ref[PLANES * side + n, pl.ds(z + 1, wide_x, stride=PAD_Z), :] = plane
            if side == 0:
                for n, plane in enumerate(coords + [held.astype(jnp.float32)]):
                    points_ref[n, pl.ds(z, CXL, stride=LZ), :] = plane[1 : CXL + 1]

    turn_ref[...] = jnp.zeros(turn_ref.shape, jnp.float32)
    tables = [[], []]
    for x in range(CXL):
        rest = jnp.concatenate([points_ref[c, x * LZ : (x + 1) * LZ, :] for c in range(3)], axis=0)
        for part in range(PARTS):
            rounded = rest.astype(jnp.bfloat16).astype(jnp.float32)
            turn_ref[CHOICE * part : CHOICE * (part + 1), :] = rounded
            rest = rest - rounded
        turned = jnp.transpose(turn_ref[...]).astype(jnp.bfloat16)
        for y in range(CYL):
            tables[y].append(turned[PPL * y : PPL * (y + 1)])
    tables = [jnp.concatenate(table, axis=0) for table in tables]
    row = lax.broadcasted_iota(jnp.int32, (LANES, LANES), 0)
    row = jnp.where(row < PARTS * CHOICE, row % CHOICE, -1)
    for z in range(LZ):
        chosen = jnp.concatenate(
            [(row == c * LZ + z).astype(jnp.float32) for c in range(3)], axis=1
        ).astype(jnp.bfloat16)
        for y in range(CYL):
            place_ref[y, z] = jnp.dot(tables[y], chosen, preferred_element_type=jnp.float32)

    def add_tiles(leaf, step):
        x = leaf // LZ
        z = leaf % LZ
        targets = []
        for u in range(STEP):
            start = pl.multiple_of(x * PPL + 8 * (STEP * step + u), 8)
            low, high = [
                [
                    place_ref[y, z, pl.ds(start, 8), LANES * c : LANES * (c + 1)]
                    for c in range(3)
                ]
                for y in range(CYL)
            ]
            for place in (low, high):
                place.append(square(place[0]) + square(place[1]) + square(place[2]))
            mixed = [jnp.where(lower_half, l, h) for l, h in zip(low, high)]
            targets.append((low, high, mixed))
        sums = [[None] * 3 for _ in range(STEP)]
        for shift_x in range(3):
            for shift_z in range(3):
                row = (x + shift_x) * PAD_Z + z + shift_z
                for side in range(2):
                    mx, my, mz, norm, weight = [
                        wide(source_ref[PLANES * side + c, pl.ds(row, 1), :]) for c in range(PLANES)
                    ]
                    for u in range(STEP):
                        for n in (0, 1) if side == 0 else (2,):
                            tx, ty, tz, own_norm = targets[u][n]
                            d2 = (own_norm + norm) + tx * mx + ty * my + tz * mz
                            value = weight * lax.rsqrt(d2)
                            if side == 0 and shift_x == 1 and shift_z == 1:
                                itself = lanes == slots + (8 * (STEP * step + u) + PPL * n)
                                value = jnp.where(itself, 0.0, value)
                            old = sums[u][n]
                            sums[u][n] = value if old is None else old + value
        for u in range(STEP):
            low, high, mixed = sums[u]
            start = pl.multiple_of(8 * (STEP * step + u), 8)
            sum_ref[leaf, pl.ds(start, 8), :] = low + jnp.where(lower_half, mixed, 0.0)
            sum_ref[leaf, pl.ds(PPL + start, 8), :] = high + jnp.where(lower_half, 0.0, mixed)

    def one_leaf_pair(leaf, carry):
        x = leaf // LZ
        z = leaf % LZ
        held = jnp.maximum(fill_ref[x, 0, z], fill_ref[x, 1, z])

        def more(step, inner):
            add_tiles(leaf, step)
            return inner

        lax.fori_loop(0, (held + 8 * STEP - 1) // (8 * STEP), more, 0)
        return carry

    lax.fori_loop(0, LEAVES, one_leaf_pair, 0)
    ones = jnp.ones((2 * LANES, LANES), jnp.bfloat16)
    diagonal = lax.broadcasted_iota(jnp.int32, (LANES, LANES), 0) == lax.broadcasted_iota(
        jnp.int32, (LANES, LANES), 1
    )

    def finish(group, carry):
        rows = []
        for n in range(8):
            whole = sum_ref[8 * group + n]
            coarse = whole.astype(jnp.bfloat16)
            fine = (whole - coarse.astype(jnp.float32)).astype(jnp.bfloat16)
            added = jnp.dot(
                jnp.concatenate([coarse, fine], axis=1), ones, preferred_element_type=jnp.float32
            )
            rows.append(jnp.sum(jnp.where(diagonal, added, 0.0), axis=0, keepdims=True))
        out_ref[pl.ds(pl.multiple_of(8 * group, 8), 8), :] = jnp.concatenate(rows, axis=0)
        return carry

    lax.fori_loop(0, LEAVES // 8, finish, 0)


def near_sums(fill, table):
    return pl.pallas_call(
        near_kernel,
        out_shape=(
            jax.ShapeDtypeStruct((LEAVES, LANES), jnp.float32),
            jax.ShapeDtypeStruct((4, LEAVES, LANES), jnp.float32),
        ),
        in_specs=[
            pl.BlockSpec(memory_space=pltpu.SMEM),
            pl.BlockSpec(memory_space=pltpu.VMEM),
        ],
        out_specs=(
            pl.BlockSpec(memory_space=pltpu.VMEM),
            pl.BlockSpec(memory_space=pltpu.VMEM),
        ),
        scratch_shapes=[
            pltpu.VMEM((2 * PLANES, (CXL + 2) * PAD_Z, LANES), jnp.float32),
            pltpu.VMEM((LEAVES, LANES, LANES), jnp.float32),
            pltpu.VMEM((LANES, LANES), jnp.float32),
            pltpu.VMEM((CYL, LZ, CXL * PPL, 3 * LANES), jnp.float32),
        ],
        compiler_params=pltpu.CompilerParams(vmem_limit_bytes=28 * 2**20),
        name="near_sums",
    )(fill, table)


def swapped(axis, head, tail):
    count = lax.axis_size(axis)
    even = lax.axis_index(axis) & 1 == 0
    first = [(i, i ^ 1) for i in range(count)]
    second = [(i, i + 1 if i % 2 else i - 1) for i in range(1, count - 1)]
    outside = lax.ppermute(jnp.where(even, head, tail), axis, second)
    inside = lax.ppermute(jnp.where(even, tail, head), axis, first)
    return jnp.where(even, outside, inside), jnp.where(even, inside, outside)


def per_device(positions, charges, counts, up_ops, m2l_ops, down_ops, box_lists):
    devices_x = lax.axis_size("gx")
    devices_y = lax.axis_size("gy")
    filled = jnp.pad(counts.astype(jnp.float32), ((0, 0), (0, 0), (0, SLOTS - LZ)))
    own = jnp.concatenate([positions, charges[None], filled[None]], axis=0).transpose(2, 0, 1, 3)
    before, after = swapped("gx", own[:, :, :1], own[:, :, -1:])
    first = one_check(1, own)
    middle = jnp.concatenate([before, own, after], axis=2)
    middle, first, own = lax.optimization_barrier((middle, first, own))
    below, above = swapped("gy", middle[:1], middle[1:])
    second = one_check(2, own)
    below, above, second, own = lax.optimization_barrier((below, above, second, own))
    sent = send_panels(
        box_lists.T, first, second, own, up_ops, m2l_ops, down_ops, devices_x, devices_y
    )
    parts = lax.all_to_all(sent, ("gx", "gy"), split_axis=0, concat_axis=0, tiled=True)
    near, points = near_sums(counts, jnp.concatenate([below, middle, above], axis=0))
    return far_and_sum(points, near, parts)


def solution(mesh):
    return jax.shard_map(
        per_device,
        mesh=mesh,
        in_specs=(
            P(None, "gx", "gy", None),
            P("gx", "gy", None),
            P("gx", "gy", None),
            P(),
            P(),
            P(),
            P(),
        ),
        out_specs=P("gx", "gy", None),
        check_vma=False,
    )
```

```python
import functools
import jax
import jax.numpy as jnp
import numpy as np
from jax import lax
from jax.experimental import pallas as pl
from jax.experimental.pallas import tpu as pltpu
from jax.sharding import PartitionSpec as P

CXL = 8
CYL = 2
LZ = 8
PPL = 64
P_ORD = 8
K = 8
LEV = 3
NE = 296
SLOTS = LZ * PPL
LANES = 128
GRANT = 52
UNROLL = 4
ROWS = CXL * CYL * SLOTS // LANES
SOFTENING = 0.01
SURFACE_REACH = 1.05
PRECISE = lax.Precision.HIGHEST
LATTICE = np.linspace(-1.0, 1.0, P_ORD)
CHUNKS = ((0, 128), (128, 256), (256, NE))
INNER = range(1, P_ORD - 1)
ENDS = (0, P_ORD - 1)
A_TILES = [(a, b) for a in ENDS for b in range(P_ORD)]
B_TILES = [(a, b) for b in ENDS for a in INNER]
C_TILES = [(b, c) for c in ENDS for b in INNER]


def first_row(a, b):
    if a == 0:
        return 8 * b
    if a == P_ORD - 1:
        return 232 + 8 * b
    return 64 + 28 * (a - 1) + (0 if b == 0 else 20)


def strided_rows(b, c):
    return pl.ds(64 + 8 + 2 * (b - 1) + (1 if c else 0), P_ORD - 2, stride=28)


def lattice_y(h):
    index_y = lax.axis_index("gy")
    base = (((index_y >> h) << h) - index_y) * CYL
    span = CYL * 2**h
    return [
        base.astype(jnp.float32)
        + float(0.5 * span * (1.0 + SURFACE_REACH * LATTICE[b]) - 0.5 * CYL)
        for b in range(P_ORD)
    ]


def wide(row):
    return jnp.broadcast_to(row, (8, LANES))


def lattice_x(a):
    return float(SURFACE_REACH * 0.5 * CXL * LATTICE[a])


def lattice_z(c):
    return float(SURFACE_REACH * 0.5 * LZ * LATTICE[c])


def along_sublanes(half):
    steps = lax.broadcasted_iota(jnp.int32, (8, LANES), 0).astype(jnp.float32)
    return steps * (SURFACE_REACH * half * 2.0 / (P_ORD - 1)) - SURFACE_REACH * half


def square(value):
    return value * value


def a_squares(x8, z8, y_parts):
    along_z = square(along_sublanes(0.5 * LZ) - z8) + SOFTENING
    for a in ENDS:
        base = square(lattice_x(a) - x8) + along_z
        for b in range(P_ORD):
            yield base + y_parts[b]


def bc_squares(x8, z8, y_parts):
    along_z = square(along_sublanes(0.5 * LZ) - z8) + SOFTENING
    bases = [square(lattice_x(a) - x8) + along_z for a in INNER]
    for b in ENDS:
        for base in bases:
            yield base + y_parts[b]
    along_x = square(along_sublanes(0.5 * CXL) - x8) + SOFTENING
    for c in ENDS:
        base = along_x + square(lattice_z(c) - z8)
        for b in INNER:
            yield base + y_parts[b]


def row_of(p_ref, r):
    return [wide(p_ref[c, pl.ds(r, 1), :]) for c in range(p_ref.shape[0])]


def fill_points(own_ref, p_ref):
    lane = lax.broadcasted_iota(jnp.int32, (CXL, LANES), 1)
    upper = lane // PPL
    slot = (lane % PPL).astype(jnp.float32)
    along_x = lax.broadcasted_iota(jnp.int32, (CXL, LANES), 0) - CXL // 2
    for y in range(CYL):
        for q in range(SLOTS // LANES):
            here = slice(LANES * q, LANES * (q + 1))
            rows = slice(CXL * (4 * y + q), CXL * (4 * y + q + 1))
            place_z = (upper + (2 * q - LZ // 2)).astype(jnp.float32)
            p_ref[0, rows, :] = own_ref[y, 0, :, here] + along_x.astype(jnp.float32)
            p_ref[1, rows, :] = own_ref[y, 1, :, here] + float(y - CYL // 2)
            p_ref[2, rows, :] = own_ref[y, 2, :, here] + place_z
            held = [
                jnp.broadcast_to(own_ref[y, 4, :, z : z + 1], (CXL, LANES))
                for z in (2 * q, 2 * q + 1)
            ]
            held = jnp.where(upper == 0, held[0], held[1])
            p_ref[3, rows, :] = jnp.where(slot < held, own_ref[y, 3, :, here], 0.0)


def add_checks(levels, p_ref, check_ref):
    for n, h in enumerate(levels):
        ys = lattice_y(h)
        tiles = A_TILES + B_TILES + C_TILES

        def gather(r, sums):
            x8, y8, z8, w8 = row_of(p_ref, r)
            y_parts = [square(ys[b] - y8) for b in range(P_ORD)]
            gaps = list(a_squares(x8, z8, y_parts)) + list(bc_squares(x8, z8, y_parts))
            return [total + w8 * lax.rsqrt(d2) for total, d2 in zip(sums, gaps)]

        sums = lax.fori_loop(
            0, ROWS, gather, [jnp.zeros((8, LANES), jnp.float32) for _ in tiles], unroll=UNROLL
        )
        for i, (total, tile) in enumerate(zip(sums, tiles)):
            filled = jnp.broadcast_to(jnp.sum(total, axis=1, keepdims=True), (8, LANES))
            if i >= len(A_TILES + B_TILES):
                check_ref[n, strided_rows(*tile), :] = filled[1:7]
            else:
                check_ref[n, pl.ds(first_row(*tile), 8), :] = filled


def check_kernel(h, own_ref, check_ref, p_ref):
    fill_points(own_ref, p_ref)
    add_checks([h], p_ref, check_ref)


def one_check(h, own):
    return pl.pallas_call(
        functools.partial(check_kernel, h),
        out_shape=jax.ShapeDtypeStruct((1, NE, LANES), jnp.float32),
        in_specs=[pl.BlockSpec(memory_space=pltpu.VMEM)],
        out_specs=pl.BlockSpec(memory_space=pltpu.VMEM),
        scratch_shapes=[pltpu.VMEM((4, ROWS, LANES), jnp.float32)],
        compiler_params=pltpu.CompilerParams(vmem_limit_bytes=4 * 2**20),
        name="one_check",
    )(own)


def halves(value):
    coarse = value.astype(jnp.bfloat16)
    return coarse, (value - coarse.astype(jnp.float32)).astype(jnp.bfloat16)


def product(rows, matrix):
    coarse, fine = halves(rows)
    count = rows.shape[0]
    wide_part, narrow_part = halves(matrix)
    both = jnp.concatenate([coarse.astype(jnp.float32), fine.astype(jnp.float32)], axis=0)
    both = jnp.dot(
        both.astype(jnp.bfloat16), wide_part, preferred_element_type=jnp.float32
    )
    rest = jnp.dot(coarse, narrow_part, preferred_element_type=jnp.float32)
    return both[:count] + (both[count:] + rest)


def send_kernel(
    span_x, span_y, lists_ref, first_ref, second_ref, own_ref, up_hbm, m2l_hbm, down_hbm,
    out_ref, p_ref, up_ref, m2l_ref, down_ref, check_ref, row_ref, column_ref, panel_ref, sems,
):
    up_copy = pltpu.make_async_copy(up_hbm, up_ref, sems.at[0])
    down_copy = pltpu.make_async_copy(down_hbm, down_ref, sems.at[1])
    level_copies = [
        pltpu.make_async_copy(m2l_hbm.at[h], m2l_ref.at[h], sems.at[2 + h]) for h in range(LEV)
    ]
    copies = [up_copy, level_copies[2], down_copy, level_copies[1], level_copies[0]]
    for copy in copies:
        copy.start()
    row_ref[...] = jnp.zeros((8, 384), jnp.float32)
    fill_points(own_ref, p_ref)
    add_checks([LEV], p_ref, check_ref)
    up_copy.wait()
    for h in range(LEV):
        for low, high in CHUNKS:
            total = jnp.zeros((8, high - low), jnp.float32)
            for i in range(0, NE, 8):
                check = (first_ref, second_ref, check_ref)[h][0, i : i + 8, : high - low]
                total += check * up_ref[h, i : i + 8, low:high]
            row_ref[h : h + 1, low:high] = jnp.sum(total, axis=0, keepdims=True)
    flipped = jnp.transpose(row_ref[...])
    for h in range(LEV):
        column_ref[h] = jnp.broadcast_to(flipped[:NE, h : h + 1], (NE, LANES))

    out_ref[...] = jnp.zeros(out_ref.shape, jnp.float32)
    index_x = lax.axis_index("gx")
    index_y = lax.axis_index("gy")

    def translated(h):
        level_copies[h].wait()

        def translate(k, carry):
            for low, high in CHUNKS:
                total = jnp.zeros((8, high - low), jnp.float32)
                for i in range(0, NE, 8):
                    total += (
                        column_ref[h, i : i + 8, : high - low]
                        * m2l_ref[h, k, i : i + 8, low:high]
                    )
                panel_ref[h, k, :, low:high] = total
            return carry

        lax.fori_loop(0, K, translate, 0)
        return jnp.sum(panel_ref[h], axis=1)

    def spread(h, row_for):
        offset = span_x * (span_y - (span_y >> h - 1))
        across = span_y >> h
        bits = across.bit_length() - 1
        own_box = (index_x << bits) + (index_y >> h)
        for k in range(K):
            box = (own_box - lists_ref[k, offset]) & (span_x * across - 1)
            first = (box >> bits) * span_y + ((box & (across - 1)) << h)
            for j in range(2**h):
                out_ref[first + j] += row_for(k, j)

    top = translated(2)
    down_copy.wait()
    top = [product(top, down_ref[1, side]) for side in range(2)]
    middle = jnp.concatenate([translated(1)] + top, axis=0)
    lower = [product(middle, down_ref[0, side]) for side in range(2)]

    def second_row(k, j):
        return lower[j // 2][k : k + 1]

    def third_row(k, j):
        start = K * (1 + j // 4) + k
        return lower[j // 2 % 2][start : start + 1]

    spread(3, third_row)
    spread(2, second_row)
    low_panel = translated(0)
    spread(1, lambda k, j: low_panel[k : k + 1])


def send_panels(lists, first, second, own, up_ops, m2l_ops, down_ops, span_x, span_y):
    return pl.pallas_call(
        functools.partial(send_kernel, span_x, span_y),
        out_shape=jax.ShapeDtypeStruct((span_x * span_y, 1, NE), jnp.float32),
        in_specs=[
            pl.BlockSpec(memory_space=pltpu.SMEM),
            pl.BlockSpec(memory_space=pltpu.VMEM),
            pl.BlockSpec(memory_space=pltpu.VMEM),
            pl.BlockSpec(memory_space=pltpu.VMEM),
            pl.BlockSpec(memory_space=pltpu.HBM),
            pl.BlockSpec(memory_space=pltpu.HBM),
            pl.BlockSpec(memory_space=pltpu.HBM),
        ],
        out_specs=pl.BlockSpec(memory_space=pltpu.VMEM),
        scratch_shapes=[
            pltpu.VMEM((4, ROWS, LANES), jnp.float32),
            pltpu.VMEM((LEV, NE, NE), jnp.float32),
            pltpu.VMEM((LEV, K, NE, NE), jnp.float32),
            pltpu.VMEM((LEV - 1, 2, NE, NE), jnp.float32),
            pltpu.VMEM((1, NE, LANES), jnp.float32),
            pltpu.VMEM((8, 384), jnp.float32),
            pltpu.VMEM((LEV, NE, LANES), jnp.float32),
            pltpu.VMEM((LEV, K, 8, NE), jnp.float32),
            pltpu.SemaphoreType.DMA((LEV + 2,)),
        ],
        compiler_params=pltpu.CompilerParams(vmem_limit_bytes=GRANT * 2**20),
        name="send_panels",
    )(lists, first, second, own, up_ops, m2l_ops, down_ops)


def far_kernel(points_ref, near_ref, parts_ref, out_ref, row_ref, column_ref, tile_ref):
    row_ref[...] = jnp.zeros((8, 384), jnp.float32)
    row_ref[0:1, :NE] = jnp.sum(parts_ref[...], axis=0)
    flipped = jnp.transpose(row_ref[...])
    column_ref[...] = jnp.broadcast_to(flipped[:NE, 0:1], (NE, LANES))
    for n, tile in enumerate(A_TILES + B_TILES):
        tile_ref[n] = column_ref[pl.ds(first_row(*tile), 8), :]
    for n, tile in enumerate(C_TILES):
        n += len(A_TILES + B_TILES)
        tile_ref[n] = jnp.zeros((8, LANES), jnp.float32)
        tile_ref[n, 1:7, :] = column_ref[strided_rows(*tile), :]
    ys = lattice_y(1)
    lower_half = lax.broadcasted_iota(jnp.int32, (1, LANES), 1) < PPL

    def potential(r):
        x8, y8, z8, held = row_of(points_ref, r)
        y_parts = [square(ys[b] - y8) for b in range(P_ORD)]
        totals = [jnp.zeros((8, LANES), jnp.float32) for _ in range(4)]
        n = 0
        for squares in (a_squares, bc_squares):
            for d2 in squares(x8, z8, y_parts):
                totals[n % 4] += tile_ref[n] * lax.rsqrt(d2)
                n += 1
        far = jnp.sum(totals[0] + totals[1] + (totals[2] + totals[3]), axis=0, keepdims=True)
        return jnp.where(held[0:1] > 0, near_ref[pl.ds(r, 1), :] + far, 0.0)

    def one_x(x, carry):
        for q in range(LZ // 2):
            first = potential(x * LZ + 2 * q)
            second = potential(x * LZ + 2 * q + 1)
            here = slice(LANES * q, LANES * (q + 1))
            turned = pltpu.roll(second, PPL, 1)
            out_ref[x, 0:1, here] = jnp.where(lower_half, first, turned)
            turned = pltpu.roll(first, PPL, 1)
            out_ref[x, 1:2, here] = jnp.where(lower_half, turned, second)
        return carry

    lax.fori_loop(0, CXL, one_x, 0)


def far_and_sum(points, near, parts):
    return pl.pallas_call(
        far_kernel,
        out_shape=jax.ShapeDtypeStruct((CXL, CYL, SLOTS), jnp.float32),
        in_specs=[pl.BlockSpec(memory_space=pltpu.VMEM)] * 3,
        out_specs=pl.BlockSpec(memory_space=pltpu.VMEM),
        scratch_shapes=[
            pltpu.VMEM((8, 384), jnp.float32),
            pltpu.VMEM((NE, LANES), jnp.float32),
            pltpu.VMEM((40, 8, LANES), jnp.float32),
        ],
        compiler_params=pltpu.CompilerParams(vmem_limit_bytes=16 * 2**20),
        name="far_and_sum",
    )(points, near, parts)


PAD_Z = LZ + 2
PLANES = 5
STEP = 2
TILES = PPL // 8
LEAVES = CXL * LZ
PARTS = 3
CHOICE = 3 * LZ


def near_kernel(
    fill_ref, table_ref, out_ref, points_ref, source_ref, sum_ref, turn_ref, place_ref
):
    lanes = lax.broadcasted_iota(jnp.int32, (8, LANES), 1)
    slots = lax.broadcasted_iota(jnp.int32, (8, LANES), 0)
    lower_half = lanes < PPL
    wide_x = CXL + 2
    lane = lax.broadcasted_iota(jnp.int32, (wide_x, LANES), 1)
    lower = lane < PPL
    along_x = lax.broadcasted_iota(jnp.int32, (wide_x, LANES), 0)
    along_x = (along_x - (1 + CXL // 2)).astype(jnp.float32)
    for plane in range(2 * PLANES):
        value = 1.0 if plane % PLANES == 3 else 0.0
        source_ref[plane] = jnp.full(source_ref.shape[1:], value, jnp.float32)
    for side, (first, second) in enumerate(((1, 2), (0, 3))):
        along_y = jnp.where(lower, float(first - 2), float(second - 2))
        for z in range(LZ):
            here = slice(z // 2 * LANES, (z // 2 + 1) * LANES)

            def both(c):
                one = table_ref[first, c, :, here]
                two = table_ref[second, c, :, here]
                if z % 2:
                    one = pltpu.roll(one, PPL, 1)
                else:
                    two = pltpu.roll(two, PPL, 1)
                return jnp.where(lower, one, two)

            held = jnp.where(
                lower,
                jnp.broadcast_to(table_ref[first, 4, :, z : z + 1], (wide_x, LANES)),
                jnp.broadcast_to(table_ref[second, 4, :, z : z + 1], (wide_x, LANES)),
            )
            held = (lane % PPL).astype(jnp.float32) < held
            coords = [both(0) + along_x, both(1) + along_y, both(2) + float(z - LZ // 2)]
            norm = square(coords[0]) + square(coords[1]) + square(coords[2]) + SOFTENING
            planes = [-2.0 * coord for coord in coords]
            planes += [norm, jnp.where(held, both(3), 0.0)]
            for n, plane in enumerate(planes):
                source_ref[PLANES * side + n, pl.ds(z + 1, wide_x, stride=PAD_Z), :] = plane
            if side == 0:
                for n, plane in enumerate(coords + [held.astype(jnp.float32)]):
                    points_ref[n, pl.ds(z, CXL, stride=LZ), :] = plane[1 : CXL + 1]

    turn_ref[...] = jnp.zeros(turn_ref.shape, jnp.float32)
    tables = [[], []]
    for x in range(CXL):
        rest = jnp.concatenate([points_ref[c, x * LZ : (x + 1) * LZ, :] for c in range(3)], axis=0)
        for part in range(PARTS):
            rounded = rest.astype(jnp.bfloat16).astype(jnp.float32)
            turn_ref[CHOICE * part : CHOICE * (part + 1), :] = rounded
            rest = rest - rounded
        turned = jnp.transpose(turn_ref[...]).astype(jnp.bfloat16)
        for y in range(CYL):
            tables[y].append(turned[PPL * y : PPL * (y + 1)])
    tables = [jnp.concatenate(table, axis=0) for table in tables]
    row = lax.broadcasted_iota(jnp.int32, (LANES, LANES), 0)
    row = jnp.where(row < PARTS * CHOICE, row % CHOICE, -1)
    for z in range(LZ):
        chosen = jnp.concatenate(
            [(row == c * LZ + z).astype(jnp.float32) for c in range(3)], axis=1
        ).astype(jnp.bfloat16)
        for y in range(CYL):
            place_ref[y, z] = jnp.dot(tables[y], chosen, preferred_element_type=jnp.float32)

    def add_tiles(leaf, step):
        x = leaf // LZ
        z = leaf % LZ
        targets = []
        for u in range(STEP):
            start = pl.multiple_of(x * PPL + 8 * (STEP * step + u), 8)
            low, high = [
                [
                    place_ref[y, z, pl.ds(start, 8), LANES * c : LANES * (c + 1)]
                    for c in range(3)
                ]
                for y in range(CYL)
            ]
            for place in (low, high):
                place.append(square(place[0]) + square(place[1]) + square(place[2]))
            mixed = [jnp.where(lower_half, l, h) for l, h in zip(low, high)]
            targets.append((low, high, mixed))
        sums = [[None] * 3 for _ in range(STEP)]
        for shift_x in range(3):
            for shift_z in range(3):
                row = (x + shift_x) * PAD_Z + z + shift_z
                for side in range(2):
                    mx, my, mz, norm, weight = [
                        wide(source_ref[PLANES * side + c, pl.ds(row, 1), :]) for c in range(PLANES)
                    ]
                    for u in range(STEP):
                        for n in (0, 1) if side == 0 else (2,):
                            tx, ty, tz, own_norm = targets[u][n]
                            d2 = (own_norm + norm) + tx * mx + ty * my + tz * mz
                            value = weight * lax.rsqrt(d2)
                            if side == 0 and shift_x == 1 and shift_z == 1:
                                itself = lanes == slots + (8 * (STEP * step + u) + PPL * n)
                                value = jnp.where(itself, 0.0, value)
                            old = sums[u][n]
                            sums[u][n] = value if old is None else old + value
        for u in range(STEP):
            low, high, mixed = sums[u]
            start = pl.multiple_of(8 * (STEP * step + u), 8)
            sum_ref[leaf, pl.ds(start, 8), :] = low + jnp.where(lower_half, mixed, 0.0)
            sum_ref[leaf, pl.ds(PPL + start, 8), :] = high + jnp.where(lower_half, 0.0, mixed)

    def one_leaf_pair(leaf, carry):
        x = leaf // LZ
        z = leaf % LZ
        held = jnp.maximum(fill_ref[x, 0, z], fill_ref[x, 1, z])

        def more(step, inner):
            add_tiles(leaf, step)
            return inner

        lax.fori_loop(0, (held + 8 * STEP - 1) // (8 * STEP), more, 0)
        return carry

    lax.fori_loop(0, LEAVES, one_leaf_pair, 0)
    ones = jnp.ones((2 * LANES, LANES), jnp.bfloat16)
    diagonal = lax.broadcasted_iota(jnp.int32, (LANES, LANES), 0) == lax.broadcasted_iota(
        jnp.int32, (LANES, LANES), 1
    )

    def finish(group, carry):
        rows = []
        for n in range(8):
            whole = sum_ref[8 * group + n]
            if n % 2:
                rows.append(jnp.sum(jnp.transpose(whole), axis=0, keepdims=True))
                continue
            coarse = whole.astype(jnp.bfloat16)
            fine = (whole - coarse.astype(jnp.float32)).astype(jnp.bfloat16)
            added = jnp.dot(
                jnp.concatenate([coarse, fine], axis=1), ones, preferred_element_type=jnp.float32
            )
            rows.append(jnp.sum(jnp.where(diagonal, added, 0.0), axis=0, keepdims=True))
        out_ref[pl.ds(pl.multiple_of(8 * group, 8), 8), :] = jnp.concatenate(rows, axis=0)
        return carry

    lax.fori_loop(0, LEAVES // 8, finish, 0)


def near_sums(fill, table):
    return pl.pallas_call(
        near_kernel,
        out_shape=(
            jax.ShapeDtypeStruct((LEAVES, LANES), jnp.float32),
            jax.ShapeDtypeStruct((4, LEAVES, LANES), jnp.float32),
        ),
        in_specs=[
            pl.BlockSpec(memory_space=pltpu.SMEM),
            pl.BlockSpec(memory_space=pltpu.VMEM),
        ],
        out_specs=(
            pl.BlockSpec(memory_space=pltpu.VMEM),
            pl.BlockSpec(memory_space=pltpu.VMEM),
        ),
        scratch_shapes=[
            pltpu.VMEM((2 * PLANES, (CXL + 2) * PAD_Z, LANES), jnp.float32),
            pltpu.VMEM((LEAVES, LANES, LANES), jnp.float32),
            pltpu.VMEM((LANES, LANES), jnp.float32),
            pltpu.VMEM((CYL, LZ, CXL * PPL, 3 * LANES), jnp.float32),
        ],
        compiler_params=pltpu.CompilerParams(vmem_limit_bytes=28 * 2**20),
        name="near_sums",
    )(fill, table)


def swapped(axis, head, tail):
    count = lax.axis_size(axis)
    even = lax.axis_index(axis) & 1 == 0
    first = [(i, i ^ 1) for i in range(count)]
    second = [(i, i + 1 if i % 2 else i - 1) for i in range(1, count - 1)]
    outside = lax.ppermute(jnp.where(even, head, tail), axis, second)
    inside = lax.ppermute(jnp.where(even, tail, head), axis, first)
    return jnp.where(even, outside, inside), jnp.where(even, inside, outside)


def per_device(positions, charges, counts, up_ops, m2l_ops, down_ops, box_lists):
    devices_x = lax.axis_size("gx")
    devices_y = lax.axis_size("gy")
    filled = jnp.pad(counts.astype(jnp.float32), ((0, 0), (0, 0), (0, SLOTS - LZ)))
    own = jnp.concatenate([positions, charges[None], filled[None]], axis=0).transpose(2, 0, 1, 3)
    before, after = swapped("gx", own[:, :, :1], own[:, :, -1:])
    first = one_check(1, own)
    middle = jnp.concatenate([before, own, after], axis=2)
    middle, first, own = lax.optimization_barrier((middle, first, own))
    below, above = swapped("gy", middle[:1], middle[1:])
    second = one_check(2, own)
    below, above, second, own = lax.optimization_barrier((below, above, second, own))
    sent = send_panels(
        box_lists.T, first, second, own, up_ops, m2l_ops, down_ops, devices_x, devices_y
    )
    parts = lax.all_to_all(sent, ("gx", "gy"), split_axis=0, concat_axis=0, tiled=True)
    near, points = near_sums(counts, jnp.concatenate([below, middle, above], axis=0))
    return far_and_sum(points, near, parts)


def solution(mesh):
    return jax.shard_map(
        per_device,
        mesh=mesh,
        in_specs=(
            P(None, "gx", "gy", None),
            P("gx", "gy", None),
            P("gx", "gy", None),
            P(),
            P(),
            P(),
            P(),
        ),
        out_specs=P("gx", "gy", None),
        check_vma=False,
    )
```

```python
import functools
import jax
import jax.numpy as jnp
import numpy as np
from jax import lax
from jax.experimental import pallas as pl
from jax.experimental.pallas import tpu as pltpu
from jax.sharding import PartitionSpec as P

CXL = 8
CYL = 2
LZ = 8
PPL = 64
P_ORD = 8
K = 8
LEV = 3
NE = 296
SLOTS = LZ * PPL
LANES = 128
GRANT = 52
UNROLL = 4
ROWS = CXL * CYL * SLOTS // LANES
SOFTENING = 0.01
SURFACE_REACH = 1.05
PRECISE = lax.Precision.HIGHEST
LATTICE = np.linspace(-1.0, 1.0, P_ORD)
CHUNKS = ((0, 128), (128, 256), (256, NE))
INNER = range(1, P_ORD - 1)
ENDS = (0, P_ORD - 1)
A_TILES = [(a, b) for a in ENDS for b in range(P_ORD)]
B_TILES = [(a, b) for b in ENDS for a in INNER]
C_TILES = [(b, c) for c in ENDS for b in INNER]


def first_row(a, b):
    if a == 0:
        return 8 * b
    if a == P_ORD - 1:
        return 232 + 8 * b
    return 64 + 28 * (a - 1) + (0 if b == 0 else 20)


def strided_rows(b, c):
    return pl.ds(64 + 8 + 2 * (b - 1) + (1 if c else 0), P_ORD - 2, stride=28)


def lattice_y(h):
    index_y = lax.axis_index("gy")
    base = (((index_y >> h) << h) - index_y) * CYL
    span = CYL * 2**h
    return [
        base.astype(jnp.float32)
        + float(0.5 * span * (1.0 + SURFACE_REACH * LATTICE[b]) - 0.5 * CYL)
        for b in range(P_ORD)
    ]


def wide(row):
    return jnp.broadcast_to(row, (8, LANES))


def lattice_x(a):
    return float(SURFACE_REACH * 0.5 * CXL * LATTICE[a])


def lattice_z(c):
    return float(SURFACE_REACH * 0.5 * LZ * LATTICE[c])


def along_sublanes(half):
    steps = lax.broadcasted_iota(jnp.int32, (8, LANES), 0).astype(jnp.float32)
    return steps * (SURFACE_REACH * half * 2.0 / (P_ORD - 1)) - SURFACE_REACH * half


def square(value):
    return value * value


def a_squares(x8, z8, y_parts):
    along_z = square(along_sublanes(0.5 * LZ) - z8) + SOFTENING
    for a in ENDS:
        base = square(lattice_x(a) - x8) + along_z
        for b in range(P_ORD):
            yield base + y_parts[b]


def bc_squares(x8, z8, y_parts):
    along_z = square(along_sublanes(0.5 * LZ) - z8) + SOFTENING
    bases = [square(lattice_x(a) - x8) + along_z for a in INNER]
    for b in ENDS:
        for base in bases:
            yield base + y_parts[b]
    along_x = square(along_sublanes(0.5 * CXL) - x8) + SOFTENING
    for c in ENDS:
        base = along_x + square(lattice_z(c) - z8)
        for b in INNER:
            yield base + y_parts[b]


def row_of(p_ref, r):
    return [wide(p_ref[c, pl.ds(r, 1), :]) for c in range(p_ref.shape[0])]


def fill_points(own_ref, p_ref):
    lane = lax.broadcasted_iota(jnp.int32, (CXL, LANES), 1)
    upper = lane // PPL
    slot = (lane % PPL).astype(jnp.float32)
    along_x = lax.broadcasted_iota(jnp.int32, (CXL, LANES), 0) - CXL // 2
    for y in range(CYL):
        for q in range(SLOTS // LANES):
            here = slice(LANES * q, LANES * (q + 1))
            rows = slice(CXL * (4 * y + q), CXL * (4 * y + q + 1))
            place_z = (upper + (2 * q - LZ // 2)).astype(jnp.float32)
            p_ref[0, rows, :] = own_ref[y, 0, :, here] + along_x.astype(jnp.float32)
            p_ref[1, rows, :] = own_ref[y, 1, :, here] + float(y - CYL // 2)
            p_ref[2, rows, :] = own_ref[y, 2, :, here] + place_z
            held = [
                jnp.broadcast_to(own_ref[y, 4, :, z : z + 1], (CXL, LANES))
                for z in (2 * q, 2 * q + 1)
            ]
            held = jnp.where(upper == 0, held[0], held[1])
            p_ref[3, rows, :] = jnp.where(slot < held, own_ref[y, 3, :, here], 0.0)


def add_checks(levels, p_ref, check_ref):
    for n, h in enumerate(levels):
        ys = lattice_y(h)
        tiles = A_TILES + B_TILES + C_TILES

        def gather(r, sums):
            x8, y8, z8, w8 = row_of(p_ref, r)
            y_parts = [square(ys[b] - y8) for b in range(P_ORD)]
            gaps = list(a_squares(x8, z8, y_parts)) + list(bc_squares(x8, z8, y_parts))
            return [total + w8 * lax.rsqrt(d2) for total, d2 in zip(sums, gaps)]

        sums = lax.fori_loop(
            0, ROWS, gather, [jnp.zeros((8, LANES), jnp.float32) for _ in tiles], unroll=UNROLL
        )
        for i, (total, tile) in enumerate(zip(sums, tiles)):
            filled = jnp.broadcast_to(jnp.sum(total, axis=1, keepdims=True), (8, LANES))
            if i >= len(A_TILES + B_TILES):
                check_ref[n, strided_rows(*tile), :] = filled[1:7]
            else:
                check_ref[n, pl.ds(first_row(*tile), 8), :] = filled


def check_kernel(h, own_ref, check_ref, p_ref):
    fill_points(own_ref, p_ref)
    add_checks([h], p_ref, check_ref)


def one_check(h, own):
    return pl.pallas_call(
        functools.partial(check_kernel, h),
        out_shape=jax.ShapeDtypeStruct((1, NE, LANES), jnp.float32),
        in_specs=[pl.BlockSpec(memory_space=pltpu.VMEM)],
        out_specs=pl.BlockSpec(memory_space=pltpu.VMEM),
        scratch_shapes=[pltpu.VMEM((4, ROWS, LANES), jnp.float32)],
        compiler_params=pltpu.CompilerParams(vmem_limit_bytes=4 * 2**20),
        name="one_check",
    )(own)


def halves(value):
    coarse = value.astype(jnp.bfloat16)
    return coarse, (value - coarse.astype(jnp.float32)).astype(jnp.bfloat16)


def product(rows, matrix):
    coarse, fine = halves(rows)
    count = rows.shape[0]
    wide_part, narrow_part = halves(matrix)
    both = jnp.concatenate([coarse.astype(jnp.float32), fine.astype(jnp.float32)], axis=0)
    both = jnp.dot(
        both.astype(jnp.bfloat16), wide_part, preferred_element_type=jnp.float32
    )
    rest = jnp.dot(coarse, narrow_part, preferred_element_type=jnp.float32)
    return both[:count] + (both[count:] + rest)


def send_kernel(
    span_x, span_y, lists_ref, first_ref, second_ref, own_ref, up_hbm, m2l_hbm, down_hbm,
    out_ref, p_ref, up_ref, m2l_ref, down_ref, check_ref, row_ref, column_ref, panel_ref, sems,
):
    up_copy = pltpu.make_async_copy(up_hbm, up_ref, sems.at[0])
    down_copy = pltpu.make_async_copy(down_hbm, down_ref, sems.at[1])
    level_copies = [
        pltpu.make_async_copy(m2l_hbm.at[h], m2l_ref.at[h], sems.at[2 + h]) for h in range(LEV)
    ]
    copies = [up_copy, level_copies[2], down_copy, level_copies[1], level_copies[0]]
    for copy in copies:
        copy.start()
    row_ref[...] = jnp.zeros((8, 384), jnp.float32)
    fill_points(own_ref, p_ref)
    add_checks([LEV], p_ref, check_ref)
    up_copy.wait()
    for h in range(LEV):
        for low, high in CHUNKS:
            total = jnp.zeros((8, high - low), jnp.float32)
            for i in range(0, NE, 8):
                check = (first_ref, second_ref, check_ref)[h][0, i : i + 8, : high - low]
                total += check * up_ref[h, i : i + 8, low:high]
            row_ref[h : h + 1, low:high] = jnp.sum(total, axis=0, keepdims=True)
    flipped = jnp.transpose(row_ref[...])
    for h in range(LEV):
        column_ref[h] = jnp.broadcast_to(flipped[:NE, h : h + 1], (NE, LANES))

    out_ref[...] = jnp.zeros(out_ref.shape, jnp.float32)
    index_x = lax.axis_index("gx")
    index_y = lax.axis_index("gy")

    def translated(h):
        level_copies[h].wait()

        def translate(k, carry):
            for low, high in CHUNKS:
                total = jnp.zeros((8, high - low), jnp.float32)
                for i in range(0, NE, 8):
                    total += (
                        column_ref[h, i : i + 8, : high - low]
                        * m2l_ref[h, k, i : i + 8, low:high]
                    )
                panel_ref[h, k, :, low:high] = total
            return carry

        lax.fori_loop(0, K, translate, 0)
        return jnp.sum(panel_ref[h], axis=1)

    def spread(h, row_for):
        offset = span_x * (span_y - (span_y >> h - 1))
        across = span_y >> h
        bits = across.bit_length() - 1
        own_box = (index_x << bits) + (index_y >> h)
        for k in range(K):
            box = (own_box - lists_ref[k, offset]) & (span_x * across - 1)
            first = (box >> bits) * span_y + ((box & (across - 1)) << h)
            for j in range(2**h):
                out_ref[first + j] += row_for(k, j)

    top = translated(2)
    down_copy.wait()
    top = [product(top, down_ref[1, side]) for side in range(2)]
    middle = jnp.concatenate([translated(1)] + top, axis=0)
    lower = [product(middle, down_ref[0, side]) for side in range(2)]

    def second_row(k, j):
        return lower[j // 2][k : k + 1]

    def third_row(k, j):
        start = K * (1 + j // 4) + k
        return lower[j // 2 % 2][start : start + 1]

    spread(3, third_row)
    spread(2, second_row)
    low_panel = translated(0)
    spread(1, lambda k, j: low_panel[k : k + 1])


def send_panels(lists, first, second, own, up_ops, m2l_ops, down_ops, span_x, span_y):
    return pl.pallas_call(
        functools.partial(send_kernel, span_x, span_y),
        out_shape=jax.ShapeDtypeStruct((span_x * span_y, 1, NE), jnp.float32),
        in_specs=[
            pl.BlockSpec(memory_space=pltpu.SMEM),
            pl.BlockSpec(memory_space=pltpu.VMEM),
            pl.BlockSpec(memory_space=pltpu.VMEM),
            pl.BlockSpec(memory_space=pltpu.VMEM),
            pl.BlockSpec(memory_space=pltpu.HBM),
            pl.BlockSpec(memory_space=pltpu.HBM),
            pl.BlockSpec(memory_space=pltpu.HBM),
        ],
        out_specs=pl.BlockSpec(memory_space=pltpu.VMEM),
        scratch_shapes=[
            pltpu.VMEM((4, ROWS, LANES), jnp.float32),
            pltpu.VMEM((LEV, NE, NE), jnp.float32),
            pltpu.VMEM((LEV, K, NE, NE), jnp.float32),
            pltpu.VMEM((LEV - 1, 2, NE, NE), jnp.float32),
            pltpu.VMEM((1, NE, LANES), jnp.float32),
            pltpu.VMEM((8, 384), jnp.float32),
            pltpu.VMEM((LEV, NE, LANES), jnp.float32),
            pltpu.VMEM((LEV, K, 8, NE), jnp.float32),
            pltpu.SemaphoreType.DMA((LEV + 2,)),
        ],
        compiler_params=pltpu.CompilerParams(vmem_limit_bytes=GRANT * 2**20),
        name="send_panels",
    )(lists, first, second, own, up_ops, m2l_ops, down_ops)


def far_kernel(points_ref, near_ref, parts_ref, out_ref, row_ref, column_ref, tile_ref):
    row_ref[...] = jnp.zeros((8, 384), jnp.float32)
    row_ref[0:1, :NE] = jnp.sum(parts_ref[...], axis=0)
    flipped = jnp.transpose(row_ref[...])
    column_ref[...] = jnp.broadcast_to(flipped[:NE, 0:1], (NE, LANES))
    for n, tile in enumerate(A_TILES + B_TILES):
        tile_ref[n] = column_ref[pl.ds(first_row(*tile), 8), :]
    for n, tile in enumerate(C_TILES):
        n += len(A_TILES + B_TILES)
        tile_ref[n] = jnp.zeros((8, LANES), jnp.float32)
        tile_ref[n, 1:7, :] = column_ref[strided_rows(*tile), :]
    ys = lattice_y(1)
    lower_half = lax.broadcasted_iota(jnp.int32, (1, LANES), 1) < PPL

    def potential(r):
        x8, y8, z8, held = row_of(points_ref, r)
        y_parts = [square(ys[b] - y8) for b in range(P_ORD)]
        totals = [jnp.zeros((8, LANES), jnp.float32) for _ in range(4)]
        n = 0
        for squares in (a_squares, bc_squares):
            for d2 in squares(x8, z8, y_parts):
                totals[n % 4] += tile_ref[n] * lax.rsqrt(d2)
                n += 1
        far = jnp.sum(totals[0] + totals[1] + (totals[2] + totals[3]), axis=0, keepdims=True)
        return jnp.where(held[0:1] > 0, near_ref[pl.ds(r, 1), :] + far, 0.0)

    def one_x(x, carry):
        for q in range(LZ // 2):
            first = potential(x * LZ + 2 * q)
            second = potential(x * LZ + 2 * q + 1)
            here = slice(LANES * q, LANES * (q + 1))
            turned = pltpu.roll(second, PPL, 1)
            out_ref[x, 0:1, here] = jnp.where(lower_half, first, turned)
            turned = pltpu.roll(first, PPL, 1)
            out_ref[x, 1:2, here] = jnp.where(lower_half, turned, second)
        return carry

    lax.fori_loop(0, CXL, one_x, 0)


def far_and_sum(points, near, parts):
    return pl.pallas_call(
        far_kernel,
        out_shape=jax.ShapeDtypeStruct((CXL, CYL, SLOTS), jnp.float32),
        in_specs=[pl.BlockSpec(memory_space=pltpu.VMEM)] * 3,
        out_specs=pl.BlockSpec(memory_space=pltpu.VMEM),
        scratch_shapes=[
            pltpu.VMEM((8, 384), jnp.float32),
            pltpu.VMEM((NE, LANES), jnp.float32),
            pltpu.VMEM((40, 8, LANES), jnp.float32),
        ],
        compiler_params=pltpu.CompilerParams(vmem_limit_bytes=16 * 2**20),
        name="far_and_sum",
    )(points, near, parts)


PAD_Z = LZ + 2
PLANES = 5
STEP = 2
TILES = PPL // 8
LEAVES = CXL * LZ
PARTS = 3
PLACES = 4
CHOICE = PLACES * LZ


def near_kernel(
    fill_ref, table_ref, out_ref, points_ref, source_ref, sum_ref, turn_ref, place_ref, back_ref
):
    lanes = lax.broadcasted_iota(jnp.int32, (8, LANES), 1)
    slots = lax.broadcasted_iota(jnp.int32, (8, LANES), 0)
    lower_half = lanes < PPL
    wide_x = CXL + 2
    lane = lax.broadcasted_iota(jnp.int32, (wide_x, LANES), 1)
    lower = lane < PPL
    along_x = lax.broadcasted_iota(jnp.int32, (wide_x, LANES), 0)
    along_x = (along_x - (1 + CXL // 2)).astype(jnp.float32)
    for plane in range(2 * PLANES):
        value = 1.0 if plane % PLANES == 3 else 0.0
        source_ref[plane] = jnp.full(source_ref.shape[1:], value, jnp.float32)
    for side, (first, second) in enumerate(((1, 2), (0, 3))):
        along_y = jnp.where(lower, float(first - 2), float(second - 2))
        for z in range(LZ):
            here = slice(z // 2 * LANES, (z // 2 + 1) * LANES)

            def both(c):
                one = table_ref[first, c, :, here]
                two = table_ref[second, c, :, here]
                if z % 2:
                    one = pltpu.roll(one, PPL, 1)
                else:
                    two = pltpu.roll(two, PPL, 1)
                return jnp.where(lower, one, two)

            held = jnp.where(
                lower,
                jnp.broadcast_to(table_ref[first, 4, :, z : z + 1], (wide_x, LANES)),
                jnp.broadcast_to(table_ref[second, 4, :, z : z + 1], (wide_x, LANES)),
            )
            held = (lane % PPL).astype(jnp.float32) < held
            coords = [both(0) + along_x, both(1) + along_y, both(2) + float(z - LZ // 2)]
            norm = square(coords[0]) + square(coords[1]) + square(coords[2]) + SOFTENING
            planes = [-2.0 * coord for coord in coords]
            planes += [norm, jnp.where(held, both(3), 0.0)]
            for n, plane in enumerate(planes):
                source_ref[PLANES * side + n, pl.ds(z + 1, wide_x, stride=PAD_Z), :] = plane
            if side == 0:
                for n, plane in enumerate(coords + [held.astype(jnp.float32)]):
                    points_ref[n, pl.ds(z, CXL, stride=LZ), :] = plane[1 : CXL + 1]

    turn_ref[...] = jnp.zeros(turn_ref.shape, jnp.float32)
    back_ref[...] = jnp.zeros(back_ref.shape, jnp.float32)
    tables = [[], []]
    for x in range(CXL):
        first = (x + 1) * PAD_Z + 1
        rest = jnp.concatenate(
            [points_ref[c, x * LZ : (x + 1) * LZ, :] for c in range(3)]
            + [source_ref[4, first : first + LZ, :]],
            axis=0,
        )
        for part in range(PARTS):
            rounded = rest.astype(jnp.bfloat16).astype(jnp.float32)
            turn_ref[CHOICE * part : CHOICE * (part + 1), :] = rounded
            rest = rest - rounded
        turned = jnp.transpose(turn_ref[...]).astype(jnp.bfloat16)
        for y in range(CYL):
            tables[y].append(turned[PPL * y : PPL * (y + 1)])
    tables = [jnp.concatenate(table, axis=0) for table in tables]
    row = lax.broadcasted_iota(jnp.int32, (LANES, LANES), 0)
    row = jnp.where(row < PARTS * CHOICE, row % CHOICE, -1)
    for z in range(LZ):
        chosen = jnp.concatenate(
            [(row == c * LZ + z).astype(jnp.float32) for c in range(PLACES)], axis=1
        ).astype(jnp.bfloat16)
        for y in range(CYL):
            place_ref[y, z] = jnp.dot(tables[y], chosen, preferred_element_type=jnp.float32)

    def add_tiles(leaf, step, at_edge):
        x = leaf // LZ
        z = leaf % LZ
        targets = []
        own_weights = []
        for u in range(STEP):
            start = pl.multiple_of(x * PPL + 8 * (STEP * step + u), 8)
            low, high = [
                [
                    place_ref[y, z, pl.ds(start, 8), LANES * c : LANES * (c + 1)]
                    for c in range(PLACES)
                ]
                for y in range(CYL)
            ]
            own_weights.append([place.pop() for place in (low, high)])
            for place in (low, high):
                place.append(square(place[0]) + square(place[1]) + square(place[2]))
            mixed = [jnp.where(lower_half, l, h) for l, h in zip(low, high)]
            targets.append((low, high, mixed))
        sums = [[None] * 3 for _ in range(STEP)]

        def plus(old, value):
            return value if old is None else old + value

        for shift_x in range(3):
            for shift_z in range(3):
                row = (x + shift_x) * PAD_Z + z + shift_z
                middle = shift_x == 1 and shift_z == 1
                forward = 3 * shift_x + shift_z > 4
                for side in range(2):
                    if side == 0 and not (middle or forward or (at_edge and shift_x == 0)):
                        continue
                    mx, my, mz, norm, weight = [
                        wide(source_ref[PLANES * side + c, pl.ds(row, 1), :]) for c in range(PLANES)
                    ]
                    back = None
                    for u in range(STEP):
                        for n in (0, 1) if side == 0 else (2,):
                            tx, ty, tz, own_norm = targets[u][n]
                            d2 = (own_norm + norm) + tx * mx + ty * my + tz * mz
                            strength = lax.rsqrt(d2)
                            if side == 0 and middle:
                                itself = lanes == slots + (8 * (STEP * step + u) + PPL * n)
                                strength = jnp.where(itself, 0.0, strength)
                            sums[u][n] = plus(sums[u][n], weight * strength)
                            if side == 0 and forward:
                                back = plus(back, own_weights[u][n] * strength)
                    if back is not None:
                        back_ref[row] += back
        for u in range(STEP):
            low, high, mixed = sums[u]
            start = pl.multiple_of(8 * (STEP * step + u), 8)
            sum_ref[leaf, pl.ds(start, 8), :] = low + jnp.where(lower_half, mixed, 0.0)
            sum_ref[leaf, pl.ds(PPL + start, 8), :] = high + jnp.where(lower_half, 0.0, mixed)

    def one_leaf_pair(at_edge, leaf, carry):
        x = leaf // LZ
        z = leaf % LZ
        held = jnp.maximum(fill_ref[x, 0, z], fill_ref[x, 1, z])

        def more(step, inner):
            add_tiles(leaf, step, at_edge)
            return inner

        lax.fori_loop(0, (held + 8 * STEP - 1) // (8 * STEP), more, 0)
        return carry

    lax.fori_loop(0, LZ, functools.partial(one_leaf_pair, True), 0)
    lax.fori_loop(LZ, LEAVES, functools.partial(one_leaf_pair, False), 0)
    def finish(group, carry):
        rows = [
            jnp.sum(jnp.transpose(sum_ref[8 * group + n]), axis=0, keepdims=True)
            for n in range(8)
        ]
        back = jnp.sum(back_ref[pl.ds((group + 1) * PAD_Z + 1, LZ)], axis=1)
        out_ref[pl.ds(pl.multiple_of(8 * group, 8), 8), :] = jnp.concatenate(rows, axis=0) + back
        return carry

    lax.fori_loop(0, LEAVES // 8, finish, 0)


def near_sums(fill, table):
    return pl.pallas_call(
        near_kernel,
        out_shape=(
            jax.ShapeDtypeStruct((LEAVES, LANES), jnp.float32),
            jax.ShapeDtypeStruct((4, LEAVES, LANES), jnp.float32),
        ),
        in_specs=[
            pl.BlockSpec(memory_space=pltpu.SMEM),
            pl.BlockSpec(memory_space=pltpu.VMEM),
        ],
        out_specs=(
            pl.BlockSpec(memory_space=pltpu.VMEM),
            pl.BlockSpec(memory_space=pltpu.VMEM),
        ),
        scratch_shapes=[
            pltpu.VMEM((2 * PLANES, (CXL + 2) * PAD_Z, LANES), jnp.float32),
            pltpu.VMEM((LEAVES, LANES, LANES), jnp.float32),
            pltpu.VMEM((LANES, LANES), jnp.float32),
            pltpu.VMEM((CYL, LZ, CXL * PPL, PLACES * LANES), jnp.float32),
            pltpu.VMEM(((CXL + 2) * PAD_Z, 8, LANES), jnp.float32),
        ],
        compiler_params=pltpu.CompilerParams(vmem_limit_bytes=28 * 2**20),
        name="near_sums",
    )(fill, table)


def swapped(axis, head, tail):
    count = lax.axis_size(axis)
    even = lax.axis_index(axis) & 1 == 0
    first = [(i, i ^ 1) for i in range(count)]
    second = [(i, i + 1 if i % 2 else i - 1) for i in range(1, count - 1)]
    outside = lax.ppermute(jnp.where(even, head, tail), axis, second)
    inside = lax.ppermute(jnp.where(even, tail, head), axis, first)
    return jnp.where(even, outside, inside), jnp.where(even, inside, outside)


def per_device(positions, charges, counts, up_ops, m2l_ops, down_ops, box_lists):
    devices_x = lax.axis_size("gx")
    devices_y = lax.axis_size("gy")
    filled = jnp.pad(counts.astype(jnp.float32), ((0, 0), (0, 0), (0, SLOTS - LZ)))
    own = jnp.concatenate([positions, charges[None], filled[None]], axis=0).transpose(2, 0, 1, 3)
    before, after = swapped("gx", own[:, :, :1], own[:, :, -1:])
    first = one_check(1, own)
    middle = jnp.concatenate([before, own, after], axis=2)
    middle, first, own = lax.optimization_barrier((middle, first, own))
    below, above = swapped("gy", middle[:1], middle[1:])
    second = one_check(2, own)
    below, above, second, own = lax.optimization_barrier((below, above, second, own))
    sent = send_panels(
        box_lists.T, first, second, own, up_ops, m2l_ops, down_ops, devices_x, devices_y
    )
    parts = lax.all_to_all(sent, ("gx", "gy"), split_axis=0, concat_axis=0, tiled=True)
    near, points = near_sums(counts, jnp.concatenate([below, middle, above], axis=0))
    return far_and_sum(points, near, parts)


def solution(mesh):
    return jax.shard_map(
        per_device,
        mesh=mesh,
        in_specs=(
            P(None, "gx", "gy", None),
            P("gx", "gy", None),
            P("gx", "gy", None),
            P(),
            P(),
            P(),
            P(),
        ),
        out_specs=P("gx", "gy", None),
        check_vma=False,
    )
```

```python
import functools
import jax
import jax.numpy as jnp
import numpy as np
from jax import lax
from jax.experimental import pallas as pl
from jax.experimental.pallas import tpu as pltpu
from jax.sharding import PartitionSpec as P

CXL = 8
CYL = 2
LZ = 8
PPL = 64
P_ORD = 8
K = 8
LEV = 3
NE = 296
SLOTS = LZ * PPL
LANES = 128
GRANT = 52
WHOLE = 60
UNROLL = 4
ROWS = CXL * CYL * SLOTS // LANES
SOFTENING = 0.01
SURFACE_REACH = 1.05
PRECISE = lax.Precision.HIGHEST
LATTICE = np.linspace(-1.0, 1.0, P_ORD)
CHUNKS = ((0, 128), (128, 256), (256, NE))
INNER = range(1, P_ORD - 1)
ENDS = (0, P_ORD - 1)
A_TILES = [(a, b) for a in ENDS for b in range(P_ORD)]
B_TILES = [(a, b) for b in ENDS for a in INNER]
C_TILES = [(b, c) for c in ENDS for b in INNER]


def first_row(a, b):
    if a == 0:
        return 8 * b
    if a == P_ORD - 1:
        return 232 + 8 * b
    return 64 + 28 * (a - 1) + (0 if b == 0 else 20)


def strided_rows(b, c):
    return pl.ds(64 + 8 + 2 * (b - 1) + (1 if c else 0), P_ORD - 2, stride=28)


def lattice_y(h):
    index_y = lax.axis_index("gy")
    base = (((index_y >> h) << h) - index_y) * CYL
    span = CYL * 2**h
    return [
        base.astype(jnp.float32)
        + float(0.5 * span * (1.0 + SURFACE_REACH * LATTICE[b]) - 0.5 * CYL)
        for b in range(P_ORD)
    ]


def wide(row):
    return jnp.broadcast_to(row, (8, LANES))


def lattice_x(a):
    return float(SURFACE_REACH * 0.5 * CXL * LATTICE[a])


def lattice_z(c):
    return float(SURFACE_REACH * 0.5 * LZ * LATTICE[c])


def along_sublanes(half):
    steps = lax.broadcasted_iota(jnp.int32, (8, LANES), 0).astype(jnp.float32)
    return steps * (SURFACE_REACH * half * 2.0 / (P_ORD - 1)) - SURFACE_REACH * half


def square(value):
    return value * value


def a_squares(x8, z8, y_parts):
    along_z = square(along_sublanes(0.5 * LZ) - z8) + SOFTENING
    for a in ENDS:
        base = square(lattice_x(a) - x8) + along_z
        for b in range(P_ORD):
            yield base + y_parts[b]


def bc_squares(x8, z8, y_parts):
    along_z = square(along_sublanes(0.5 * LZ) - z8) + SOFTENING
    bases = [square(lattice_x(a) - x8) + along_z for a in INNER]
    for b in ENDS:
        for base in bases:
            yield base + y_parts[b]
    along_x = square(along_sublanes(0.5 * CXL) - x8) + SOFTENING
    for c in ENDS:
        base = along_x + square(lattice_z(c) - z8)
        for b in INNER:
            yield base + y_parts[b]


def row_of(p_ref, r):
    return [wide(p_ref[c, pl.ds(r, 1), :]) for c in range(p_ref.shape[0])]


def collect_kernel(
    positions_hbm, charges_hbm, counts_hbm, own_ref, first_ref, second_ref,
    positions_ref, charges_ref, counts_ref, sems,
):
    even = lax.axis_index("gx") & 1 == 0
    copies = [
        pltpu.make_async_copy(positions_hbm, positions_ref, sems.at[0]),
        pltpu.make_async_copy(charges_hbm, charges_ref, sems.at[1]),
        pltpu.make_async_copy(counts_hbm, counts_ref, sems.at[2]),
    ]
    for copy in copies:
        copy.start()
    for copy in copies:
        copy.wait()
    for y in range(CYL):
        own_ref[y, 4] = jnp.zeros((CXL, SLOTS), jnp.float32)
        own_ref[y, 4, :, :LZ] = counts_ref[:, y, :].astype(jnp.float32)
        own_ref[y, 3] = charges_ref[:, y, :]
        for c in range(3):
            own_ref[y, c] = positions_ref[c, :, y, :]
        for c in range(5):
            head = own_ref[y, c, 0:1, :]
            tail = own_ref[y, c, CXL - 1 : CXL, :]
            first_ref[y, c] = jnp.where(even, tail, head)
            second_ref[y, c] = jnp.where(even, head, tail)


def collect(positions, charges, counts):
    face = jax.ShapeDtypeStruct((CYL, 5, 1, SLOTS), jnp.float32)
    return pl.pallas_call(
        collect_kernel,
        out_shape=(jax.ShapeDtypeStruct((CYL, 5, CXL, SLOTS), jnp.float32), face, face),
        in_specs=[pl.BlockSpec(memory_space=pltpu.HBM)] * 3,
        out_specs=(pl.BlockSpec(memory_space=pltpu.VMEM),) * 3,
        scratch_shapes=[
            pltpu.VMEM((3, CXL, CYL, SLOTS), jnp.float32),
            pltpu.VMEM((CXL, CYL, SLOTS), jnp.float32),
            pltpu.VMEM((CXL, CYL, LZ), jnp.int32),
            pltpu.SemaphoreType.DMA((3,)),
        ],
        compiler_params=pltpu.CompilerParams(vmem_limit_bytes=WHOLE * 2**20),
        name="collect",
    )(positions, charges, counts)


def fill_points(own_ref, p_ref):
    lane = lax.broadcasted_iota(jnp.int32, (CXL, LANES), 1)
    upper = lane // PPL
    slot = (lane % PPL).astype(jnp.float32)
    along_x = lax.broadcasted_iota(jnp.int32, (CXL, LANES), 0) - CXL // 2
    for y in range(CYL):
        for q in range(SLOTS // LANES):
            here = slice(LANES * q, LANES * (q + 1))
            rows = slice(CXL * (4 * y + q), CXL * (4 * y + q + 1))
            place_z = (upper + (2 * q - LZ // 2)).astype(jnp.float32)
            p_ref[0, rows, :] = own_ref[y, 0, :, here] + along_x.astype(jnp.float32)
            p_ref[1, rows, :] = own_ref[y, 1, :, here] + float(y - CYL // 2)
            p_ref[2, rows, :] = own_ref[y, 2, :, here] + place_z
            held = [
                jnp.broadcast_to(own_ref[y, 4, :, z : z + 1], (CXL, LANES))
                for z in (2 * q, 2 * q + 1)
            ]
            held = jnp.where(upper == 0, held[0], held[1])
            p_ref[3, rows, :] = jnp.where(slot < held, own_ref[y, 3, :, here], 0.0)


def add_checks(levels, p_ref, check_ref):
    for n, h in enumerate(levels):
        ys = lattice_y(h)
        tiles = A_TILES + B_TILES + C_TILES

        def gather(r, sums):
            x8, y8, z8, w8 = row_of(p_ref, r)
            y_parts = [square(ys[b] - y8) for b in range(P_ORD)]
            gaps = list(a_squares(x8, z8, y_parts)) + list(bc_squares(x8, z8, y_parts))
            return [total + w8 * lax.rsqrt(d2) for total, d2 in zip(sums, gaps)]

        sums = lax.fori_loop(
            0, ROWS, gather, [jnp.zeros((8, LANES), jnp.float32) for _ in tiles], unroll=UNROLL
        )
        for i, (total, tile) in enumerate(zip(sums, tiles)):
            filled = jnp.broadcast_to(jnp.sum(total, axis=1, keepdims=True), (8, LANES))
            if i >= len(A_TILES + B_TILES):
                check_ref[n, strided_rows(*tile), :] = filled[1:7]
            else:
                check_ref[n, pl.ds(first_row(*tile), 8), :] = filled


def check_kernel(h, own_ref, check_ref, p_ref):
    fill_points(own_ref, p_ref)
    add_checks([h], p_ref, check_ref)


def one_check(h, own):
    return pl.pallas_call(
        functools.partial(check_kernel, h),
        out_shape=jax.ShapeDtypeStruct((1, NE, LANES), jnp.float32),
        in_specs=[pl.BlockSpec(memory_space=pltpu.VMEM)],
        out_specs=pl.BlockSpec(memory_space=pltpu.VMEM),
        scratch_shapes=[pltpu.VMEM((4, ROWS, LANES), jnp.float32)],
        compiler_params=pltpu.CompilerParams(vmem_limit_bytes=4 * 2**20),
        name="one_check",
    )(own)


def halves(value):
    coarse = value.astype(jnp.bfloat16)
    return coarse, (value - coarse.astype(jnp.float32)).astype(jnp.bfloat16)


def product(rows, matrix):
    coarse, fine = halves(rows)
    count = rows.shape[0]
    wide_part, narrow_part = halves(matrix)
    both = jnp.concatenate([coarse.astype(jnp.float32), fine.astype(jnp.float32)], axis=0)
    both = jnp.dot(
        both.astype(jnp.bfloat16), wide_part, preferred_element_type=jnp.float32
    )
    rest = jnp.dot(coarse, narrow_part, preferred_element_type=jnp.float32)
    return both[:count] + (both[count:] + rest)


def send_kernel(
    span_x, span_y, lists_ref, first_ref, second_ref, own_ref, up_hbm, m2l_hbm, down_hbm,
    out_ref, p_ref, up_ref, m2l_ref, down_ref, check_ref, row_ref, column_ref, panel_ref, sems,
):
    up_copy = pltpu.make_async_copy(up_hbm, up_ref, sems.at[0])
    down_copy = pltpu.make_async_copy(down_hbm, down_ref, sems.at[1])
    level_copies = [
        pltpu.make_async_copy(m2l_hbm.at[h], m2l_ref.at[h], sems.at[2 + h]) for h in range(LEV)
    ]
    copies = [up_copy, level_copies[2], down_copy, level_copies[1], level_copies[0]]
    for copy in copies:
        copy.start()
    row_ref[...] = jnp.zeros((8, 384), jnp.float32)
    fill_points(own_ref, p_ref)
    add_checks([LEV], p_ref, check_ref)
    up_copy.wait()
    for h in range(LEV):
        for low, high in CHUNKS:
            total = jnp.zeros((8, high - low), jnp.float32)
            for i in range(0, NE, 8):
                check = (first_ref, second_ref, check_ref)[h][0, i : i + 8, : high - low]
                total += check * up_ref[h, i : i + 8, low:high]
            row_ref[h : h + 1, low:high] = jnp.sum(total, axis=0, keepdims=True)
    flipped = jnp.transpose(row_ref[...])
    for h in range(LEV):
        column_ref[h] = jnp.broadcast_to(flipped[:NE, h : h + 1], (NE, LANES))

    out_ref[...] = jnp.zeros(out_ref.shape, jnp.float32)
    index_x = lax.axis_index("gx")
    index_y = lax.axis_index("gy")

    def translated(h):
        level_copies[h].wait()

        def translate(k, carry):
            for low, high in CHUNKS:
                total = jnp.zeros((8, high - low), jnp.float32)
                for i in range(0, NE, 8):
                    total += (
                        column_ref[h, i : i + 8, : high - low]
                        * m2l_ref[h, k, i : i + 8, low:high]
                    )
                panel_ref[h, k, :, low:high] = total
            return carry

        lax.fori_loop(0, K, translate, 0)
        return jnp.sum(panel_ref[h], axis=1)

    def spread(h, row_for):
        offset = span_x * (span_y - (span_y >> h - 1))
        across = span_y >> h
        bits = across.bit_length() - 1
        own_box = (index_x << bits) + (index_y >> h)
        for k in range(K):
            box = (own_box - lists_ref[k, offset]) & (span_x * across - 1)
            first = (box >> bits) * span_y + ((box & (across - 1)) << h)
            for j in range(2**h):
                out_ref[first + j] += row_for(k, j)

    top = translated(2)
    down_copy.wait()
    top = [product(top, down_ref[1, side]) for side in range(2)]
    middle = jnp.concatenate([translated(1)] + top, axis=0)
    lower = [product(middle, down_ref[0, side]) for side in range(2)]

    def second_row(k, j):
        return lower[j // 2][k : k + 1]

    def third_row(k, j):
        start = K * (1 + j // 4) + k
        return lower[j // 2 % 2][start : start + 1]

    spread(3, third_row)
    spread(2, second_row)
    low_panel = translated(0)
    spread(1, lambda k, j: low_panel[k : k + 1])


def send_panels(lists, first, second, own, up_ops, m2l_ops, down_ops, span_x, span_y):
    return pl.pallas_call(
        functools.partial(send_kernel, span_x, span_y),
        out_shape=jax.ShapeDtypeStruct((span_x * span_y, 1, NE), jnp.float32),
        in_specs=[
            pl.BlockSpec(memory_space=pltpu.SMEM),
            pl.BlockSpec(memory_space=pltpu.VMEM),
            pl.BlockSpec(memory_space=pltpu.VMEM),
            pl.BlockSpec(memory_space=pltpu.VMEM),
            pl.BlockSpec(memory_space=pltpu.HBM),
            pl.BlockSpec(memory_space=pltpu.HBM),
            pl.BlockSpec(memory_space=pltpu.HBM),
        ],
        out_specs=pl.BlockSpec(memory_space=pltpu.VMEM),
        scratch_shapes=[
            pltpu.VMEM((4, ROWS, LANES), jnp.float32),
            pltpu.VMEM((LEV, NE, NE), jnp.float32),
            pltpu.VMEM((LEV, K, NE, NE), jnp.float32),
            pltpu.VMEM((LEV - 1, 2, NE, NE), jnp.float32),
            pltpu.VMEM((1, NE, LANES), jnp.float32),
            pltpu.VMEM((8, 384), jnp.float32),
            pltpu.VMEM((LEV, NE, LANES), jnp.float32),
            pltpu.VMEM((LEV, K, 8, NE), jnp.float32),
            pltpu.SemaphoreType.DMA((LEV + 2,)),
        ],
        compiler_params=pltpu.CompilerParams(vmem_limit_bytes=GRANT * 2**20),
        name="send_panels",
    )(lists, first, second, own, up_ops, m2l_ops, down_ops)


def far_kernel(points_ref, near_ref, parts_ref, out_ref, row_ref, column_ref, tile_ref):
    row_ref[...] = jnp.zeros((8, 384), jnp.float32)
    row_ref[0:1, :NE] = jnp.sum(parts_ref[...], axis=0)
    flipped = jnp.transpose(row_ref[...])
    column_ref[...] = jnp.broadcast_to(flipped[:NE, 0:1], (NE, LANES))
    for n, tile in enumerate(A_TILES + B_TILES):
        tile_ref[n] = column_ref[pl.ds(first_row(*tile), 8), :]
    for n, tile in enumerate(C_TILES):
        n += len(A_TILES + B_TILES)
        tile_ref[n] = jnp.zeros((8, LANES), jnp.float32)
        tile_ref[n, 1:7, :] = column_ref[strided_rows(*tile), :]
    ys = lattice_y(1)
    lower_half = lax.broadcasted_iota(jnp.int32, (1, LANES), 1) < PPL

    def potential(r):
        x8, y8, z8, held = row_of(points_ref, r)
        y_parts = [square(ys[b] - y8) for b in range(P_ORD)]
        totals = [jnp.zeros((8, LANES), jnp.float32) for _ in range(4)]
        n = 0
        for squares in (a_squares, bc_squares):
            for d2 in squares(x8, z8, y_parts):
                totals[n % 4] += tile_ref[n] * lax.rsqrt(d2)
                n += 1
        far = jnp.sum(totals[0] + totals[1] + (totals[2] + totals[3]), axis=0, keepdims=True)
        return jnp.where(held[0:1] > 0, near_ref[pl.ds(r, 1), :] + far, 0.0)

    def one_x(x, carry):
        for q in range(LZ // 2):
            first = potential(x * LZ + 2 * q)
            second = potential(x * LZ + 2 * q + 1)
            here = slice(LANES * q, LANES * (q + 1))
            turned = pltpu.roll(second, PPL, 1)
            out_ref[x, 0:1, here] = jnp.where(lower_half, first, turned)
            turned = pltpu.roll(first, PPL, 1)
            out_ref[x, 1:2, here] = jnp.where(lower_half, turned, second)
        return carry

    lax.fori_loop(0, CXL, one_x, 0)


def far_and_sum(points, near, parts):
    return pl.pallas_call(
        far_kernel,
        out_shape=jax.ShapeDtypeStruct((CXL, CYL, SLOTS), jnp.float32),
        in_specs=[pl.BlockSpec(memory_space=pltpu.VMEM)] * 3,
        out_specs=pl.BlockSpec(memory_space=pltpu.VMEM),
        scratch_shapes=[
            pltpu.VMEM((8, 384), jnp.float32),
            pltpu.VMEM((NE, LANES), jnp.float32),
            pltpu.VMEM((40, 8, LANES), jnp.float32),
        ],
        compiler_params=pltpu.CompilerParams(vmem_limit_bytes=16 * 2**20),
        name="far_and_sum",
    )(points, near, parts)


PAD_Z = LZ + 2
PLANES = 5
STEP = 2
TILES = PPL // 8
LEAVES = CXL * LZ
PARTS = 3
PLACES = 4
CHOICE = PLACES * LZ


def near_kernel(
    fill_ref, table_ref, out_ref, points_ref, source_ref, sum_ref, turn_ref, place_ref, back_ref
):
    lanes = lax.broadcasted_iota(jnp.int32, (8, LANES), 1)
    slots = lax.broadcasted_iota(jnp.int32, (8, LANES), 0)
    lower_half = lanes < PPL
    wide_x = CXL + 2
    lane = lax.broadcasted_iota(jnp.int32, (wide_x, LANES), 1)
    lower = lane < PPL
    along_x = lax.broadcasted_iota(jnp.int32, (wide_x, LANES), 0)
    along_x = (along_x - (1 + CXL // 2)).astype(jnp.float32)
    for plane in range(2 * PLANES):
        value = 1.0 if plane % PLANES == 3 else 0.0
        source_ref[plane] = jnp.full(source_ref.shape[1:], value, jnp.float32)
    for side, (first, second) in enumerate(((1, 2), (0, 3))):
        along_y = jnp.where(lower, float(first - 2), float(second - 2))
        for z in range(LZ):
            here = slice(z // 2 * LANES, (z // 2 + 1) * LANES)

            def both(c):
                one = table_ref[first, c, :, here]
                two = table_ref[second, c, :, here]
                if z % 2:
                    one = pltpu.roll(one, PPL, 1)
                else:
                    two = pltpu.roll(two, PPL, 1)
                return jnp.where(lower, one, two)

            held = jnp.where(
                lower,
                jnp.broadcast_to(table_ref[first, 4, :, z : z + 1], (wide_x, LANES)),
                jnp.broadcast_to(table_ref[second, 4, :, z : z + 1], (wide_x, LANES)),
            )
            held = (lane % PPL).astype(jnp.float32) < held
            coords = [both(0) + along_x, both(1) + along_y, both(2) + float(z - LZ // 2)]
            norm = square(coords[0]) + square(coords[1]) + square(coords[2]) + SOFTENING
            planes = [-2.0 * coord for coord in coords]
            planes += [norm, jnp.where(held, both(3), 0.0)]
            for n, plane in enumerate(planes):
                source_ref[PLANES * side + n, pl.ds(z + 1, wide_x, stride=PAD_Z), :] = plane
            if side == 0:
                for n, plane in enumerate(coords + [held.astype(jnp.float32)]):
                    points_ref[n, pl.ds(z, CXL, stride=LZ), :] = plane[1 : CXL + 1]

    turn_ref[...] = jnp.zeros(turn_ref.shape, jnp.float32)
    back_ref[...] = jnp.zeros(back_ref.shape, jnp.float32)
    tables = [[], []]
    for x in range(CXL):
        first = (x + 1) * PAD_Z + 1
        rest = jnp.concatenate(
            [points_ref[c, x * LZ : (x + 1) * LZ, :] for c in range(3)]
            + [source_ref[4, first : first + LZ, :]],
            axis=0,
        )
        for part in range(PARTS):
            rounded = rest.astype(jnp.bfloat16).astype(jnp.float32)
            turn_ref[CHOICE * part : CHOICE * (part + 1), :] = rounded
            rest = rest - rounded
        turned = jnp.transpose(turn_ref[...]).astype(jnp.bfloat16)
        for y in range(CYL):
            tables[y].append(turned[PPL * y : PPL * (y + 1)])
    tables = [jnp.concatenate(table, axis=0) for table in tables]
    row = lax.broadcasted_iota(jnp.int32, (LANES, LANES), 0)
    row = jnp.where(row < PARTS * CHOICE, row % CHOICE, -1)
    for z in range(LZ):
        chosen = jnp.concatenate(
            [(row == c * LZ + z).astype(jnp.float32) for c in range(PLACES)], axis=1
        ).astype(jnp.bfloat16)
        for y in range(CYL):
            place_ref[y, z] = jnp.dot(tables[y], chosen, preferred_element_type=jnp.float32)

    def add_tiles(leaf, step, at_edge):
        x = leaf // LZ
        z = leaf % LZ
        targets = []
        own_weights = []
        for u in range(STEP):
            start = pl.multiple_of(x * PPL + 8 * (STEP * step + u), 8)
            low, high = [
                [
                    place_ref[y, z, pl.ds(start, 8), LANES * c : LANES * (c + 1)]
                    for c in range(PLACES)
                ]
                for y in range(CYL)
            ]
            own_weights.append([place.pop() for place in (low, high)])
            for place in (low, high):
                place.append(square(place[0]) + square(place[1]) + square(place[2]))
            mixed = [jnp.where(lower_half, l, h) for l, h in zip(low, high)]
            targets.append((low, high, mixed))
        sums = [[None] * 3 for _ in range(STEP)]

        def plus(old, value):
            return value if old is None else old + value

        for shift_x in range(3):
            for shift_z in range(3):
                row = (x + shift_x) * PAD_Z + z + shift_z
                middle = shift_x == 1 and shift_z == 1
                forward = 3 * shift_x + shift_z > 4
                for side in range(2):
                    if side == 0 and not (middle or forward or (at_edge and shift_x == 0)):
                        continue
                    mx, my, mz, norm, weight = [
                        wide(source_ref[PLANES * side + c, pl.ds(row, 1), :]) for c in range(PLANES)
                    ]
                    back = None
                    for u in range(STEP):
                        for n in (0, 1) if side == 0 else (2,):
                            tx, ty, tz, own_norm = targets[u][n]
                            d2 = (own_norm + norm) + tx * mx + ty * my + tz * mz
                            strength = lax.rsqrt(d2)
                            if side == 0 and middle:
                                itself = lanes == slots + (8 * (STEP * step + u) + PPL * n)
                                strength = jnp.where(itself, 0.0, strength)
                            sums[u][n] = plus(sums[u][n], weight * strength)
                            if side == 0 and forward:
                                back = plus(back, own_weights[u][n] * strength)
                    if back is not None:
                        back_ref[row] += back
        for u in range(STEP):
            low, high, mixed = sums[u]
            start = pl.multiple_of(8 * (STEP * step + u), 8)
            sum_ref[leaf, pl.ds(start, 8), :] = low + jnp.where(lower_half, mixed, 0.0)
            sum_ref[leaf, pl.ds(PPL + start, 8), :] = high + jnp.where(lower_half, 0.0, mixed)

    def one_leaf_pair(at_edge, leaf, carry):
        x = leaf // LZ
        z = leaf % LZ
        held = jnp.maximum(fill_ref[x, 0, z], fill_ref[x, 1, z])

        def more(step, inner):
            add_tiles(leaf, step, at_edge)
            return inner

        lax.fori_loop(0, (held + 8 * STEP - 1) // (8 * STEP), more, 0)
        return carry

    lax.fori_loop(0, LZ, functools.partial(one_leaf_pair, True), 0)
    lax.fori_loop(LZ, LEAVES, functools.partial(one_leaf_pair, False), 0)
    def finish(group, carry):
        rows = [
            jnp.sum(jnp.transpose(sum_ref[8 * group + n]), axis=0, keepdims=True)
            for n in range(8)
        ]
        back = jnp.sum(back_ref[pl.ds((group + 1) * PAD_Z + 1, LZ)], axis=1)
        out_ref[pl.ds(pl.multiple_of(8 * group, 8), 8), :] = jnp.concatenate(rows, axis=0) + back
        return carry

    lax.fori_loop(0, LEAVES // 8, finish, 0)


def near_sums(fill, table):
    return pl.pallas_call(
        near_kernel,
        out_shape=(
            jax.ShapeDtypeStruct((LEAVES, LANES), jnp.float32),
            jax.ShapeDtypeStruct((4, LEAVES, LANES), jnp.float32),
        ),
        in_specs=[
            pl.BlockSpec(memory_space=pltpu.SMEM),
            pl.BlockSpec(memory_space=pltpu.VMEM),
        ],
        out_specs=(
            pl.BlockSpec(memory_space=pltpu.VMEM),
            pl.BlockSpec(memory_space=pltpu.VMEM),
        ),
        scratch_shapes=[
            pltpu.VMEM((2 * PLANES, (CXL + 2) * PAD_Z, LANES), jnp.float32),
            pltpu.VMEM((LEAVES, LANES, LANES), jnp.float32),
            pltpu.VMEM((LANES, LANES), jnp.float32),
            pltpu.VMEM((CYL, LZ, CXL * PPL, PLACES * LANES), jnp.float32),
            pltpu.VMEM(((CXL + 2) * PAD_Z, 8, LANES), jnp.float32),
        ],
        compiler_params=pltpu.CompilerParams(vmem_limit_bytes=28 * 2**20),
        name="near_sums",
    )(fill, table)


def swapped(axis, for_first, for_second):
    count = lax.axis_size(axis)
    even = lax.axis_index(axis) & 1 == 0
    first = [(i, i ^ 1) for i in range(count)]
    second = [(i, i + 1 if i % 2 else i - 1) for i in range(1, count - 1)]
    inside = lax.ppermute(for_first, axis, first)
    outside = lax.ppermute(for_second, axis, second)
    return jnp.where(even, outside, inside), jnp.where(even, inside, outside)


def per_device(positions, charges, counts, up_ops, m2l_ops, down_ops, box_lists):
    devices_x = lax.axis_size("gx")
    devices_y = lax.axis_size("gy")
    own, for_first, for_second = collect(positions, charges, counts)
    before, after = swapped("gx", for_first, for_second)
    first = one_check(1, own)
    before, after, first, own = lax.optimization_barrier((before, after, first, own))
    even = lax.axis_index("gy") & 1 == 0
    head, tail = [
        jnp.concatenate([side[y : y + 1] for side in (before, own, after)], axis=2)
        for y in range(CYL)
    ]
    below, above = swapped("gy", jnp.where(even, tail, head), jnp.where(even, head, tail))
    second = one_check(2, own)
    below, above, second, own = lax.optimization_barrier((below, above, second, own))
    sent = send_panels(
        box_lists.T, first, second, own, up_ops, m2l_ops, down_ops, devices_x, devices_y
    )
    parts = lax.all_to_all(sent, ("gx", "gy"), split_axis=0, concat_axis=0, tiled=True)
    near, points = near_sums(counts, jnp.concatenate([below, head, tail, above], axis=0))
    return far_and_sum(points, near, parts)


def solution(mesh):
    return jax.shard_map(
        per_device,
        mesh=mesh,
        in_specs=(
            P(None, "gx", "gy", None),
            P("gx", "gy", None),
            P("gx", "gy", None),
            P(),
            P(),
            P(),
            P(),
        ),
        out_specs=P("gx", "gy", None),
        check_vma=False,
    )
```
